32 devices in a mesh: tower: 2 (over core), depth: 4 (over z), sub: 4 (over y, x).
Axes of the slice: x: 2, y: 2, z: 4, core: 2. Of those that a mesh axis runs over, the one named last changes fastest.
Arguments:
- embeds: bfloat16 [2, 16384, 1024], P('tower', ('depth', 'sub')), may hold values from -700 to 700
- counts: int32 [16], P(('depth', 'sub')), may hold values from 256 to 1024, as said below
Outputs:
- row_grads: bfloat16 [2, 16384, 1024], P('tower', ('depth', 'sub'))
- corr_mean: float32 [], replicated
The draws below stay inside these ranges and needn't reach their ends.
Inputs may be any that keep to these rules, and one draw needn't show every extreme that they name: `counts`: block b holds at least 256 and at most 256 + 768 * b // 15 valid samples; the first block holds exactly 256 and the last block is full.
All inputs are finite; a program needn't handle non-finite values.
Results may differ from the reference program's by a relative error of at most 0.022.
Values may be sent and summed in bfloat16 or wider, within the bound.
No kernel may reach another device: no remote copies, remote signals or barrier semaphores. Data moves between devices by JAX's collectives and lax.ppermute only.
A program may use at most 128 MiB of HBM per device.

```python
import math
import jax
import jax.numpy as jnp
from jax import lax

O = 1024
ROWS_DEV = 1024
BLOCKS = 16
SAMPLES = 16384


def draw_embeds(key, part):
    keys_list = [jax.random.fold_in(key, 11 + step) for step in range(6)]
    shared = jax.random.truncated_normal(keys_list[0], -4.0, 4.0, (SAMPLES, O), jnp.float32)
    noise_pair = jax.random.truncated_normal(keys_list[1], -4.0, 4.0, (2, SAMPLES, O), jnp.float32)
    row_low = 0.5
    row_high = 2.0
    log_part = 0.8 * shared + 0.6 * noise_pair[0]
    image_part = 0.5 * shared + 0.5 * jnp.roll(shared, 37, axis=1) + 0.7 * noise_pair[1]
    stacked = jnp.stack([log_part, image_part])
    column_scale = jnp.exp(jax.random.uniform(keys_list[3], (2, 1, O), jnp.float32, math.log(0.3), math.log(3.0)))
    row_scale = jnp.exp(jax.random.uniform(keys_list[4], (1, SAMPLES, 1), jnp.float32, math.log(row_low), math.log(row_high)))
    block_index = (jnp.arange(SAMPLES, dtype=jnp.int32) // ROWS_DEV).astype(jnp.float32)
    depth_ramp = jnp.exp(math.log(12.0) * block_index / max(BLOCKS - 1, 1))
    return (stacked * column_scale * row_scale * depth_ramp[None, :, None]).astype(jnp.bfloat16)


def draw_counts(key, part):
    block_index = jnp.arange(BLOCKS, dtype=jnp.int32)
    upper_bound = ROWS_DEV // 4 + 1 + 3 * ROWS_DEV // 4 * block_index // max(BLOCKS - 1, 1)
    drawn_counts = jax.random.randint(jax.random.fold_in(key, 5), (BLOCKS,), ROWS_DEV // 4, upper_bound, dtype=jnp.int32)
    return jnp.where(block_index == BLOCKS - 1, ROWS_DEV, drawn_counts).astype(jnp.int32)


def setup_inputs(seed: int = 0) -> dict:
    key_list = jax.random.split(jax.random.key(seed), 3)
    embeds = draw_embeds(jax.random.fold_in(key_list[2], 71), 0)
    counts = draw_counts(jax.random.fold_in(key_list[2], 71), 0)
    return dict(embeds=embeds, counts=counts)


REG = 0.001
contract_rows = (((0,), (0,)), ((), ()))

def whitening(block_rows, valid_rows, gram_total, column_sum, count_total):
    feature_width = block_rows.shape[1]
    column_mean = column_sum / count_total
    covariance = (gram_total - jnp.outer(column_sum, column_mean)) / (count_total - 1.0) + REG * jnp.eye(feature_width, dtype=jnp.float32)
    factor_lower = jnp.linalg.cholesky(covariance)
    centered = jnp.where(valid_rows[:, None], block_rows.astype(jnp.float32) - column_mean[None, :], 0.0)
    whitened = jax.scipy.linalg.solve_triangular(factor_lower, centered.T, lower=True).T
    return (whitened.astype(jnp.bfloat16), factor_lower)

def tower_stats(block_rows, valid_rows):
    masked = jnp.where(valid_rows[:, None], block_rows, jnp.zeros_like(block_rows))
    gram_total = lax.dot_general(masked.astype(jnp.float32), masked.astype(jnp.float32), contract_rows, preferred_element_type=jnp.float32)
    column_sum = jnp.sum(masked, axis=0, dtype=jnp.float32)
    return (gram_total, column_sum)

def gradient_rows(own_white, other_white, turned, factor_lower, valid_rows):
    product_rows = jnp.dot(own_white.astype(jnp.float32), turned.astype(jnp.float32), preferred_element_type=jnp.float32)
    residual = (other_white.astype(jnp.float32) - product_rows).astype(jnp.bfloat16)
    back_rows = lax.dot_general(residual.astype(jnp.float32), turned.astype(jnp.float32), (((1,), (1,)), ((), ())), preferred_element_type=jnp.float32)
    solved = jax.scipy.linalg.solve_triangular(factor_lower, back_rows.T, lower=True, trans=1).T
    return jnp.where(valid_rows[:, None], solved, 0.0).astype(jnp.bfloat16)

def reference(embeds, counts):
    sample_count = embeds.shape[1]
    feature_width = embeds.shape[2]
    slot_index = jnp.arange(sample_count, dtype=jnp.int32)
    row_limit = jnp.repeat(counts.astype(jnp.int32), ROWS_DEV)
    valid_rows = slot_index % ROWS_DEV < row_limit
    count_total = jnp.sum(counts).astype(jnp.float32)
    log_gram, log_sum = tower_stats(embeds[0], valid_rows)
    image_gram, image_sum = tower_stats(embeds[1], valid_rows)
    log_white, log_lower = whitening(embeds[0], valid_rows, log_gram, log_sum, count_total)
    image_white, image_lower = whitening(embeds[1], valid_rows, image_gram, image_sum, count_total)
    cross = lax.dot_general(log_white.astype(jnp.float32), image_white.astype(jnp.float32), contract_rows, preferred_element_type=jnp.float32) / (count_total - 1.0)
    cross_bf = cross.astype(jnp.bfloat16)
    corr_mean = jnp.sum(jnp.square(cross_bf.astype(jnp.float32))) / feature_width
    log_grad = gradient_rows(log_white, image_white, cross_bf, log_lower, valid_rows)
    image_grad = gradient_rows(image_white, log_white, cross_bf.T, image_lower, valid_rows)
    return (jnp.stack([log_grad, image_grad]), corr_mean)
```

```python
import jax
import jax.numpy as jnp
from jax import lax
from jax.experimental import pallas as pl
from jax.experimental.pallas import tpu as pltpu
from jax.sharding import PartitionSpec as P

REG = 0.001
LEAF = 128
F32 = jnp.float32
BF16 = jnp.bfloat16
VMEM_LIMIT = 56 << 20


def shift_perm(size, apart):
    return [(source, (source + apart) % size) for source in range(size)]


def bit_perm(size, mask):
    return [(source, source ^ mask) for source in range(size)]


def halving_masks(size):
    return [1 << b for b in range(size.bit_length() - 1)]


def halve(value, axis, mask):
    half = value.shape[0] // 2
    upper = (lax.axis_index(axis) // mask) % 2
    keep = lax.dynamic_slice_in_dim(value, upper * half, half, 0)
    give = lax.dynamic_slice_in_dim(value, (1 - upper) * half, half, 0)
    return keep + lax.ppermute(give, axis, bit_perm(lax.axis_size(axis), mask))


def unhalve(value, axis, mask):
    upper = (lax.axis_index(axis) // mask) % 2
    other = lax.ppermute(value, axis, bit_perm(lax.axis_size(axis), mask))
    first = jnp.where(upper == 0, value, other)
    second = jnp.where(upper == 0, other, value)
    return jnp.concatenate([first, second], axis=0)


def scatter_direct(value, axis):
    size = lax.axis_size(axis)
    me = lax.axis_index(axis)
    part = value.shape[0] // size
    total = lax.dynamic_slice_in_dim(value, me * part, part, 0)
    for apart in range(1, size):
        give = lax.dynamic_slice_in_dim(value, ((me + apart) % size) * part, part, 0)
        total = total + lax.ppermute(give, axis, shift_perm(size, apart))
    return total


def gather_direct(value, axis):
    size = lax.axis_size(axis)
    me = lax.axis_index(axis)
    part = value.shape[0]
    out = jnp.zeros((size * part,) + value.shape[1:], value.dtype)
    out = lax.dynamic_update_slice_in_dim(out, value, me * part, 0)
    for apart in range(1, size):
        got = lax.ppermute(value, axis, shift_perm(size, apart))
        out = lax.dynamic_update_slice_in_dim(out, got, ((me - apart) % size) * part, 0)
    return out


def all_sum_pieces(value):
    masks = halving_masks(lax.axis_size("sub"))
    half = value.shape[0] // 2
    pieces = []
    for piece, order in ((value[:half], masks), (value[half:], masks[::-1])):
        for mask in order:
            piece = halve(piece, "sub", mask)
        if lax.axis_size("depth") <= 4:
            piece = scatter_direct(piece, "depth")
            piece = gather_direct(piece, "depth")
        else:
            for mask in halving_masks(lax.axis_size("depth")):
                piece = halve(piece, "depth", mask)
            for mask in halving_masks(lax.axis_size("depth"))[::-1]:
                piece = unhalve(piece, "depth", mask)
        for mask in order[::-1]:
            piece = unhalve(piece, "sub", mask)
        pieces.append(piece)
    return pieces


def split(x):
    hi = x.astype(BF16)
    return hi, (x - hi.astype(F32)).astype(BF16)


def dot(a, b, dims=((1,), (0,))):
    return lax.dot_general(a, b, (dims, ((), ())), preferred_element_type=F32)


def dot3(a, b):
    (ah, al), (bh, bl) = split(a), split(b)
    return dot(ah, bh) + (dot(ah, bl) + dot(al, bh))


def full(shape, dtype):
    return jax.ShapeDtypeStruct(shape, dtype)


def smem():
    return pl.BlockSpec(memory_space=pltpu.SMEM)


def vmem():
    return pl.BlockSpec(memory_space=pltpu.VMEM)


def call(kernel, out_shape, n_smem, n_vmem, scratch=()):
    return pl.pallas_call(
        kernel,
        out_shape=out_shape,
        in_specs=[smem()] * n_smem + [vmem()] * n_vmem,
        out_specs=jax.tree.map(lambda _: vmem(), out_shape),
        scratch_shapes=list(scratch),
        compiler_params=pltpu.CompilerParams(vmem_limit_bytes=VMEM_LIMIT),
    )


def gram_kernel(count_ref, x_ref, out_ref, masked_ref):
    rows, width = x_ref.shape
    blocks = width // LEAF
    count = count_ref[0]
    valid = lax.broadcasted_iota(jnp.int32, (rows, LEAF), 0) < count
    for j in range(blocks):
        cols = pl.ds(j * LEAF, LEAF)
        masked_ref[:, cols] = jnp.where(valid, x_ref[:, cols].astype(F32), 0.0).astype(BF16)
    sums = dot(jnp.ones((8, rows), BF16), masked_ref[...])
    sub = lax.broadcasted_iota(jnp.int32, (LEAF, LEAF), 0)
    lane = lax.broadcasted_iota(jnp.int32, (LEAF, LEAF), 1)
    for i in range(blocks):
        wide = (i + 1) * LEAF
        strip = dot(masked_ref[:, i * LEAF : wide], masked_ref[:, :wide], ((0,), (0,)))
        tile = strip[:, i * LEAF :]
        mine = sums[0:1, i * LEAF : wide]
        tile = jnp.where((sub == 0) & (lane > 0), mine, tile)
        last = lane == LEAF - 1
        tile = jnp.where((sub == 1) & last, mine[:, 0:1], tile)
        tile = jnp.where((sub == 2) & last, count.astype(F32), tile)
        if i >= blocks // 2:
            at, row = 0, blocks - 1 - i
        else:
            at, row = (blocks - i) * LEAF, i
        here = pl.ds(row * LEAF, LEAF)
        if i:
            out_ref[here, at : at + i * LEAF] = strip[:, : i * LEAF]
        out_ref[here, at + i * LEAF : at + wide] = tile


def cross_kernel(tower_ref, count_ref, own_ref, other_ref, out_ref):
    rows, width = own_ref.shape
    half = width // 2
    valid = lax.broadcasted_iota(jnp.int32, (rows, half), 0) < count_ref[0]

    def part(left_ref, right_ref, first):
        left = left_ref[:, first : first + half]
        left = jnp.where(valid, left.astype(F32), 0.0).astype(BF16)
        out_ref[...] = dot(left, right_ref[...], ((0,), (0,)))

    @pl.when(tower_ref[0] == 0)
    def _():
        part(own_ref, other_ref, 0)

    @pl.when(tower_ref[0] != 0)
    def _():
        part(other_ref, own_ref, half)


def inverse_two(a, b, d):
    scale = 1.0 / (a * d - b * b)
    return d * scale, -b * scale, a * scale


def inverse_four(p):
    e00, e01, e11 = inverse_two(p[0][0], p[0][1], p[1][1])
    b00, b01, b10, b11 = p[0][2], p[0][3], p[1][2], p[1][3]
    f00, f01 = e00 * b00 + e01 * b10, e00 * b01 + e01 * b11
    f10, f11 = e01 * b00 + e11 * b10, e01 * b01 + e11 * b11
    g00, g01, g11 = inverse_two(
        p[2][2] - (b00 * f00 + b10 * f10),
        p[2][3] - (b00 * f01 + b10 * f11),
        p[3][3] - (b01 * f01 + b11 * f11),
    )
    h00, h01 = -(f00 * g00 + f01 * g01), -(f00 * g01 + f01 * g11)
    h10, h11 = -(f10 * g00 + f11 * g01), -(f10 * g01 + f11 * g11)
    q00 = e00 - (h00 * f00 + h01 * f01)
    q01 = e01 - (h00 * f10 + h01 * f11)
    q11 = e11 - (h10 * f10 + h11 * f11)
    return [
        [q00, q01, h00, h01],
        [q01, q11, h10, h11],
        [h00, h10, g00, g01],
        [h01, h11, g01, g11],
    ]


PIVOT = 4


def leaf_inverse(block):
    size = block.shape[0]
    tiles = [block[8 * i : 8 * i + 8, :] for i in range(size // 8)]
    lane = lax.broadcasted_iota(jnp.int32, (8, size), 1)
    sub = lax.broadcasted_iota(jnp.int32, (8, size), 0)
    lane1 = lane[0:1]
    for first in range(0, size, PIVOT):
        home, row = first // 8, first % 8
        span = range(PIVOT)
        rows = [tiles[home][row + a : row + a + 1, :] for a in span]
        cols = [
            [jnp.broadcast_to(t[:, first + b : first + b + 1], (8, size)) for t in tiles]
            for b in span
        ]
        pivot = [[cols[b][home][row + a : row + a + 1, :] for b in span] for a in span]
        inv = inverse_four(pivot)
        inside1 = (lane1 >= first) & (lane1 < first + PIVOT)
        rows = [
            jnp.where(inside1, jnp.where(lane1 == first + a, 1.0, 0.0), rows[a]) for a in span
        ]
        scaled = []
        for a in span:
            acc = inv[a][0] * rows[0]
            for b in range(1, PIVOT):
                acc = acc + inv[a][b] * rows[b]
            scaled.append(jnp.broadcast_to(acc, (8, size)))
        inside = (lane >= first) & (lane < first + PIVOT)
        fresh = []
        for i, tile in enumerate(tiles):
            acc = jnp.where(inside, 0.0, tile)
            for a in span:
                acc = acc - cols[a][i] * scaled[a]
            if i == home:
                for a in span:
                    acc = jnp.where(sub == row + a, scaled[a], acc)
            fresh.append(acc)
        tiles = fresh
    return jnp.concatenate(tiles, axis=0)


def inverse_kernel(top_ref, low_ref, out_ref, sums_ref, panel_ref):
    width = out_ref.shape[0]
    blocks = width // LEAF
    per = top_ref.shape[0] // LEAF
    sub = lax.broadcasted_iota(jnp.int32, (LEAF, LEAF), 0)
    lane = lax.broadcasted_iota(jnp.int32, (LEAF, LEAF), 1)

    def packed(i):
        row = blocks - 1 - i if i >= blocks // 2 else i
        at = 0 if i >= blocks // 2 else (blocks - i) * LEAF
        ref = top_ref if row < per else low_ref
        return ref, pl.ds((row % per) * LEAF, LEAF), at

    for i in range(blocks):
        ref, here, at = packed(i)
        tile = ref[here, at + i * LEAF : at + (i + 1) * LEAF]
        first = tile[1:2, LEAF - 1 : LEAF]
        mine = jnp.where(lane[0:1] == 0, first, tile[0:1, :])
        sums_ref[0:1, i * LEAF : (i + 1) * LEAF] = mine
        if i == 0:
            count = jnp.broadcast_to(tile[2:3, LEAF - 1 : LEAF], (1, LEAF))
    wide_count = jnp.concatenate([count] * blocks, axis=1)
    sums_ref[1:2, :] = wide_count
    sums_ref[2:3, :] = sums_ref[0:1, :] / wide_count
    sums_ref[3:8, :] = jnp.zeros((5, width), F32)
    scale = 1.0 / (count - 1.0)
    means = sums_ref[2:3, :]
    for i in range(blocks):
        ref, here, at = packed(i)
        own = pl.ds(i * LEAF, LEAF)
        column = jnp.transpose(jnp.broadcast_to(sums_ref[0:1, i * LEAF : (i + 1) * LEAF], (LEAF, LEAF)))
        for j in range(i + 1):
            tile = ref[here, at + j * LEAF : at + (j + 1) * LEAF]
            if j == i:
                tile = jnp.where(sub >= lane, tile, jnp.transpose(tile))
            tile = (tile - column * means[:, j * LEAF : (j + 1) * LEAF]) * scale
            if j == i:
                tile = tile + jnp.where(sub == lane, REG, 0.0)
            out_ref[own, j * LEAF : (j + 1) * LEAF] = tile
            if j < i:
                out_ref[pl.ds(j * LEAF, LEAF), i * LEAF : (i + 1) * LEAF] = jnp.transpose(tile)

    def step(k, carry):
        here = pl.ds(pl.multiple_of(k * LEAF, LEAF), LEAF)
        inv = leaf_inverse(out_ref[here, here])
        panel_ref[...] = out_ref[:, here]
        out_ref[:, here] = jnp.zeros((width, LEAF), F32)
        out_ref[here, here] = jnp.where(sub == lane, 1.0, 0.0)
        strip = dot3(inv, out_ref[here, :])
        panel_ref[here, :] = jnp.zeros((LEAF, LEAF), F32)
        for i in range(0, width, 256):
            out_ref[i : i + 256, :] = out_ref[i : i + 256, :] - dot3(panel_ref[i : i + 256, :], strip)
        out_ref[here, :] = strip
        return carry

    lax.fori_loop(0, blocks, step, 0)


def regress_kernel(tower_ref, inv_ref, low_ref, high_ref, sums_ref, other_ref, hi_ref, lo_ref, s_ref):
    width = inv_ref.shape[0]
    half = width // 2
    count = sums_ref[1:2, :]
    scale = 1.0 / (count - 1.0)

    def centre(left_sums, right_mean):
        for i in range(0, width, LEAF):
            ref = low_ref if i < half else high_ref
            rows = pl.ds(i % half, LEAF)
            column = jnp.transpose(jnp.broadcast_to(left_sums[:, i : i + LEAF], (LEAF, LEAF)))
            for j in range(0, width, LEAF):
                tile = ref[rows, j : j + LEAF] - column * right_mean[:, j : j + LEAF]
                s_ref[i : i + LEAF, j : j + LEAF] = tile * scale[:, j : j + LEAF]

    @pl.when(tower_ref[0] == 0)
    def _():
        centre(sums_ref[0:1, :], other_ref[2:3, :])

    @pl.when(tower_ref[0] != 0)
    def _():
        centre(other_ref[0:1, :], sums_ref[2:3, :])
        for i in range(0, width, LEAF):
            for j in range(0, i + LEAF, LEAF):
                a = jnp.transpose(s_ref[i : i + LEAF, j : j + LEAF])
                if j == i:
                    s_ref[i : i + LEAF, i : i + LEAF] = a
                else:
                    b = jnp.transpose(s_ref[j : j + LEAF, i : i + LEAF])
                    s_ref[i : i + LEAF, j : j + LEAF] = b
                    s_ref[j : j + LEAF, i : i + LEAF] = a

    sh, sl = split(s_ref[...])
    for i in range(0, width, 256):
        ah, al = split(inv_ref[i : i + 256, :])
        k = dot(ah, sh) + (dot(ah, sl) + dot(al, sh))
        hi, lo = split(k)
        hi_ref[i : i + 256, :] = hi
        lo_ref[i : i + 256, :] = lo


def residual_kernel(count_ref, own_ref, other_ref, sums_ref, osums_ref, hi_ref, lo_ref, out_ref):
    rows, width = own_ref.shape
    mean_hi, mean_lo = split(jnp.broadcast_to(sums_ref[2:3, :], (8, width)))
    shift = dot(mean_hi, hi_ref[...]) + (dot(mean_hi, lo_ref[...]) + dot(mean_lo, hi_ref[...]))
    shift = shift[0:1, :] - osums_ref[2:3, :]
    for i in range(0, rows, 256):
        x = own_ref[i : i + 256, :]
        fit = dot(x, hi_ref[...]) + dot(x, lo_ref[...])
        res = other_ref[i : i + 256, :].astype(F32) - fit + shift
        valid = i + lax.broadcasted_iota(jnp.int32, (256, width), 0) < count_ref[0]
        out_ref[i : i + 256, :] = jnp.where(valid, res, 0.0).astype(BF16)


def gradient_kernel(res_ref, inv_ref, hi_ref, lo_ref, ohi_ref, olo_ref, out_ref, corr_ref, mh_ref, ml_ref):
    rows, width = res_ref.shape
    ih, il = split(inv_ref[...])
    corr_ref[...] = jnp.zeros((8, LEAF), F32)
    for i in range(0, width, 256):
        kh, kl = ohi_ref[i : i + 256, :], olo_ref[i : i + 256, :]
        mh, ml = split(dot(kh, ih) + (dot(kh, il) + dot(kl, ih)))
        mh_ref[i : i + 256, :] = mh
        ml_ref[i : i + 256, :] = ml
    for i in range(0, rows, 256):
        r = res_ref[i : i + 256, :]
        out_ref[i : i + 256, :] = (dot(r, mh_ref[...]) + dot(r, ml_ref[...])).astype(BF16)
    total = jnp.zeros((LEAF, LEAF), F32)
    for i in range(0, width, LEAF):
        for j in range(0, width, LEAF):
            a = hi_ref[i : i + LEAF, j : j + LEAF].astype(F32) + lo_ref[i : i + LEAF, j : j + LEAF].astype(F32)
            b = ohi_ref[j : j + LEAF, i : i + LEAF].astype(F32) + olo_ref[j : j + LEAF, i : i + LEAF].astype(F32)
            total = total + a * jnp.transpose(b)
    corr_ref[...] = jnp.broadcast_to(jnp.sum(total), (8, LEAF)) / width


def on_device(embeds, counts):
    own = embeds[0]
    rows, width = own.shape
    tower = lax.axis_index("tower").astype(jnp.int32)
    tower_arr = tower.reshape(1)
    swap = bit_perm(lax.axis_size("tower"), 1)
    other = lax.ppermute(own, "tower", swap)
    blocks = width // LEAF
    packed_shape = (width // 2, (blocks + 1) * LEAF)
    packed = call(gram_kernel, full(packed_shape, F32), 1, 1, [pltpu.VMEM((rows, width), BF16)])(counts, own)
    cross = call(cross_kernel, full((width // 2, width), F32), 2, 2)(tower_arr, counts, own, other)
    top, low = all_sum_pieces(packed)
    inv, sums = call(
        inverse_kernel,
        (full((width, width), F32), full((8, width), F32)),
        0,
        2,
        [pltpu.VMEM((width, LEAF), F32)],
    )(top, low)
    other_sums = lax.ppermute(sums, "tower", swap)
    my_half = jnp.concatenate(all_sum_pieces(cross), axis=0)
    their_half = lax.ppermute(my_half, "tower", swap)
    first_half = jnp.where(tower == 0, my_half, their_half)
    second_half = jnp.where(tower == 0, their_half, my_half)
    square = full((width, width), BF16)
    hi, lo = call(regress_kernel, (square, square), 1, 5, [pltpu.VMEM((width, width), F32)])(
        tower_arr, inv, first_half, second_half, sums, other_sums
    )
    other_hi = lax.ppermute(hi, "tower", swap)
    other_lo = lax.ppermute(lo, "tower", swap)
    res = call(residual_kernel, full((rows, width), BF16), 1, 6)(counts, own, other, sums, other_sums, hi, lo)
    grad, corr = call(
        gradient_kernel,
        (full((rows, width), BF16), full((8, LEAF), F32)),
        0,
        6,
        [pltpu.VMEM((width, width), BF16)] * 2,
    )(res, inv, hi, lo, other_hi, other_lo)
    shared = lax.ppermute(corr, "tower", [(0, t) for t in range(1, lax.axis_size("tower"))])
    corr_mean = jnp.where(tower == 0, corr, shared)[0, 0]
    return grad[None], corr_mean


def solution(mesh):
    placed = (P("tower", ("depth", "sub"), None), P(("depth", "sub")))
    return jax.shard_map(
        on_device,
        mesh=mesh,
        in_specs=placed,
        out_specs=(P("tower", ("depth", "sub"), None), P()),
        check_vma=False,
    )
```

```python
import functools

import jax
import jax.numpy as jnp
from jax import lax
from jax.experimental import pallas as pl
from jax.experimental.pallas import tpu as pltpu
from jax.sharding import PartitionSpec as P

REG = 0.001
LEAF = 128
F32 = jnp.float32
BF16 = jnp.bfloat16
VMEM_LIMIT = 40 << 20


def shift_perm(size, apart):
    return [(source, (source + apart) % size) for source in range(size)]


def bit_perm(size, mask):
    return [(source, source ^ mask) for source in range(size)]


def halving_masks(size):
    return [1 << b for b in range(size.bit_length() - 1)]


def swap_all(pieces, axis):
    size = lax.axis_size(axis)
    return [lax.ppermute(pieces[d], axis, bit_perm(size, d)) for d in range(1, size)]


def spread(piece, axis):
    size = lax.axis_size(axis)
    return [piece] + [lax.ppermute(piece, axis, bit_perm(size, d)) for d in range(1, size)]


def index_of(axis):
    return lax.axis_index(axis).astype(jnp.int32).reshape(1)


def tie(first, then):
    return lax.optimization_barrier((first, then))


def sum_split(own, got, axis):
    size = lax.axis_size(axis)
    rows, wide = own.shape
    part = full((rows // size, wide), F32)
    return list(call(split_kernel, (part,) * size, 1, 1 + len(got))(index_of(axis), own, *got))


def total(own, got):
    return call(total_kernel, full(own.shape, F32), 0, 1 + len(got))(own, *got)


def join(pieces, axis):
    rows, wide = pieces[0].shape
    whole = full((rows * len(pieces), wide), F32)
    return call(join_kernel, whole, 1, len(pieces))(index_of(axis), *pieces)


def split(x):
    hi = x.astype(BF16)
    return hi, (x - hi.astype(F32)).astype(BF16)


def dot(a, b, dims=((1,), (0,))):
    return lax.dot_general(a, b, (dims, ((), ())), preferred_element_type=F32)


def dot3(a, b):
    (ah, al), (bh, bl) = split(a), split(b)
    return dot(ah, bh) + (dot(ah, bl) + dot(al, bh))


def full(shape, dtype):
    return jax.ShapeDtypeStruct(shape, dtype)


def smem():
    return pl.BlockSpec(memory_space=pltpu.SMEM)


def vmem():
    return pl.BlockSpec(memory_space=pltpu.VMEM)


def call(kernel, out_shape, n_smem, n_vmem, scratch=()):
    return pl.pallas_call(
        kernel,
        out_shape=out_shape,
        in_specs=[smem()] * n_smem + [vmem()] * n_vmem,
        out_specs=jax.tree.map(lambda _: vmem(), out_shape),
        scratch_shapes=list(scratch),
        compiler_params=pltpu.CompilerParams(vmem_limit_bytes=VMEM_LIMIT),
    )


def split_kernel(me_ref, *refs):
    outs = [ref for ref in refs if ref.shape[0] != refs[0].shape[0]]
    ins = refs[: len(refs) - len(outs)]
    rows = outs[0].shape[0]
    for d, out_ref in enumerate(outs):
        here = pl.ds(pl.multiple_of((me_ref[0] ^ d) * rows, rows), rows)
        acc = ins[0][here, :]
        for ref in ins[1:]:
            acc = acc + ref[here, :]
        out_ref[...] = acc


def total_kernel(*refs):
    acc = refs[0][...]
    for ref in refs[1:-1]:
        acc = acc + ref[...]
    refs[-1][...] = acc


def join_kernel(me_ref, *refs):
    rows = refs[0].shape[0]
    for d, ref in enumerate(refs[:-1]):
        refs[-1][pl.ds(pl.multiple_of((me_ref[0] ^ d) * rows, rows), rows), :] = ref[...]


def deal(me, source_ref, outs):
    rows = outs[0].shape[0]
    for d, out_ref in enumerate(outs):
        out_ref[...] = source_ref[pl.ds(pl.multiple_of((me ^ d) * rows, rows), rows), :]


def gram_kernel(me_ref, count_ref, x_ref, *refs):
    outs, masked_ref, out_ref = refs[:-2], refs[-2], refs[-1]
    rows, width = x_ref.shape
    blocks = width // LEAF
    count = count_ref[0]
    valid = lax.broadcasted_iota(jnp.int32, (rows, LEAF), 0) < count
    for j in range(blocks):
        cols = pl.ds(j * LEAF, LEAF)
        masked_ref[:, cols] = jnp.where(valid, x_ref[:, cols].astype(F32), 0.0).astype(BF16)
    sums = dot(jnp.ones((8, rows), BF16), masked_ref[...])
    sub = lax.broadcasted_iota(jnp.int32, (LEAF, LEAF), 0)
    lane = lax.broadcasted_iota(jnp.int32, (LEAF, LEAF), 1)
    for i in range(blocks):
        wide = (i + 1) * LEAF
        strip = dot(masked_ref[:, i * LEAF : wide], masked_ref[:, :wide], ((0,), (0,)))
        tile = strip[:, i * LEAF :]
        mine = sums[0:1, i * LEAF : wide]
        tile = jnp.where((sub == 0) & (lane > 0), mine, tile)
        last = lane == LEAF - 1
        tile = jnp.where((sub == 1) & last, mine[:, 0:1], tile)
        tile = jnp.where((sub == 2) & last, count.astype(F32), tile)
        if i >= blocks // 2:
            at, row = 0, blocks - 1 - i
        else:
            at, row = (blocks - i) * LEAF, i
        here = pl.ds(row * LEAF, LEAF)
        if i:
            out_ref[here, at : at + i * LEAF] = strip[:, : i * LEAF]
        out_ref[here, at + i * LEAF : at + wide] = tile
    deal(me_ref[0], out_ref, outs)


def cross_kernel(me_ref, tower_ref, count_ref, own_ref, other_ref, *refs):
    outs, out_ref = refs[:-1], refs[-1]
    rows, width = own_ref.shape
    half = width // 2
    valid = lax.broadcasted_iota(jnp.int32, (rows, half), 0) < count_ref[0]

    def part(left_ref, right_ref, first):
        left = left_ref[:, first : first + half]
        left = jnp.where(valid, left.astype(F32), 0.0).astype(BF16)
        out_ref[...] = dot(left, right_ref[...], ((0,), (0,)))

    @pl.when(tower_ref[0] == 0)
    def _():
        part(own_ref, other_ref, 0)

    @pl.when(tower_ref[0] != 0)
    def _():
        part(other_ref, own_ref, half)

    deal(me_ref[0], out_ref, outs)


def inverse_two(a, b, d):
    scale = 1.0 / (a * d - b * b)
    return d * scale, -b * scale, a * scale


def inverse_four(p):
    e00, e01, e11 = inverse_two(p[0][0], p[0][1], p[1][1])
    b00, b01, b10, b11 = p[0][2], p[0][3], p[1][2], p[1][3]
    f00, f01 = e00 * b00 + e01 * b10, e00 * b01 + e01 * b11
    f10, f11 = e01 * b00 + e11 * b10, e01 * b01 + e11 * b11
    g00, g01, g11 = inverse_two(
        p[2][2] - (b00 * f00 + b10 * f10),
        p[2][3] - (b00 * f01 + b10 * f11),
        p[3][3] - (b01 * f01 + b11 * f11),
    )
    h00, h01 = -(f00 * g00 + f01 * g01), -(f00 * g01 + f01 * g11)
    h10, h11 = -(f10 * g00 + f11 * g01), -(f10 * g01 + f11 * g11)
    q00 = e00 - (h00 * f00 + h01 * f01)
    q01 = e01 - (h00 * f10 + h01 * f11)
    q11 = e11 - (h10 * f10 + h11 * f11)
    return [
        [q00, q01, h00, h01],
        [q01, q11, h10, h11],
        [h00, h10, g00, g01],
        [h01, h11, g01, g11],
    ]


PIVOT = 4


def leaf_inverse(block):
    size = block.shape[0]
    tile = (8, size)
    tiles = [block[8 * i : 8 * i + 8, :] for i in range(size // 8)]
    lane = lax.broadcasted_iota(jnp.int32, tile, 1)
    sub = lax.broadcasted_iota(jnp.int32, tile, 0)
    span = range(PIVOT)
    for first in range(0, size, PIVOT):
        home, row = first // 8, first % 8
        rows = [jnp.broadcast_to(tiles[home][row + a : row + a + 1, :], tile) for a in span]
        pivot = [[None] * PIVOT for _ in span]
        for a in span:
            for b in range(a, PIVOT):
                entry = jnp.broadcast_to(rows[a][:, first + b : first + b + 1], tile)
                pivot[a][b] = pivot[b][a] = entry
        cols = [
            [jnp.broadcast_to(t[:, first + b : first + b + 1], tile) for t in tiles] for b in span
        ]
        inv = inverse_four(pivot)
        inside = (lane >= first) & (lane < first + PIVOT)
        rows = [jnp.where(inside, jnp.where(lane == first + a, 1.0, 0.0), rows[a]) for a in span]
        scaled = []
        for a in span:
            acc = inv[a][0] * rows[0]
            for b in range(1, PIVOT):
                acc = acc + inv[a][b] * rows[b]
            scaled.append(acc)
        fresh = []
        for i, old in enumerate(tiles):
            acc = jnp.where(inside, 0.0, old)
            for a in span:
                acc = acc - cols[a][i] * scaled[a]
            if i == home:
                for a in span:
                    acc = jnp.where(sub == row + a, scaled[a], acc)
            fresh.append(acc)
        tiles = fresh
    return jnp.concatenate(tiles, axis=0)


def update(out_ref, panel_ref, strip_ref, prev):
    high, low = split(strip_ref[...])
    for i in range(0, out_ref.shape[0], 256):
        ph, plo = split(panel_ref[i : i + 256, :])
        product = dot(ph, high) + (dot(ph, low) + dot(plo, high))
        out_ref[i : i + 256, :] = out_ref[i : i + 256, :] - product
    out_ref[prev, :] = strip_ref[...]


def block(k):
    return pl.ds(pl.multiple_of(k * LEAF, LEAF), LEAF)


def eliminate(out_ref, panel_ref, strip_ref, first, last):
    width = out_ref.shape[0]
    sub = lax.broadcasted_iota(jnp.int32, (LEAF, LEAF), 0)
    lane = lax.broadcasted_iota(jnp.int32, (LEAF, LEAF), 1)

    def body(k, carry):
        here = block(k)
        inv = leaf_inverse(out_ref[here, here] - dot3(panel_ref[here, :], strip_ref[:, here]))
        update(out_ref, panel_ref, strip_ref, block(jnp.maximum(k - 1, 0)))
        panel_ref[...] = out_ref[:, here]
        out_ref[:, here] = jnp.zeros((width, LEAF), F32)
        out_ref[here, here] = jnp.where(sub == lane, 1.0, 0.0)
        strip_ref[...] = dot3(inv, out_ref[here, :])
        panel_ref[here, :] = jnp.zeros((LEAF, LEAF), F32)
        return carry

    lax.fori_loop(first, last, body, 0)


def begin_kernel(me_ref, *refs, steps):
    ins, (out_ref, sums_ref, panel_ref, strip_ref, packed_ref) = refs[:-5], refs[-5:]
    width = out_ref.shape[0]
    blocks = width // LEAF
    sub = lax.broadcasted_iota(jnp.int32, (LEAF, LEAF), 0)
    lane = lax.broadcasted_iota(jnp.int32, (LEAF, LEAF), 1)
    rows = ins[0].shape[0]
    for d, ref in enumerate(ins):
        packed_ref[pl.ds(pl.multiple_of((me_ref[0] ^ d) * rows, rows), rows), :] = ref[...]

    def packed(i):
        if i >= blocks // 2:
            return pl.ds((blocks - 1 - i) * LEAF, LEAF), 0
        return pl.ds(i * LEAF, LEAF), (blocks - i) * LEAF

    for i in range(blocks):
        here, at = packed(i)
        tile = packed_ref[here, at + i * LEAF : at + (i + 1) * LEAF]
        first = tile[1:2, LEAF - 1 : LEAF]
        mine = jnp.where(lane[0:1] == 0, first, tile[0:1, :])
        sums_ref[0:1, i * LEAF : (i + 1) * LEAF] = mine
        if i == 0:
            count = jnp.broadcast_to(tile[2:3, LEAF - 1 : LEAF], (1, LEAF))
    wide_count = jnp.concatenate([count] * blocks, axis=1)
    sums_ref[1:2, :] = wide_count
    sums_ref[2:3, :] = sums_ref[0:1, :] / wide_count
    sums_ref[3:8, :] = jnp.zeros((5, width), F32)
    scale = 1.0 / (count - 1.0)
    means = sums_ref[2:3, :]
    for i in range(blocks):
        here, at = packed(i)
        own = pl.ds(i * LEAF, LEAF)
        column = jnp.transpose(jnp.broadcast_to(sums_ref[0:1, i * LEAF : (i + 1) * LEAF], (LEAF, LEAF)))
        for j in range(i + 1):
            tile = packed_ref[here, at + j * LEAF : at + (j + 1) * LEAF]
            if j == i:
                tile = jnp.where(sub >= lane, tile, jnp.transpose(tile))
            tile = (tile - column * means[:, j * LEAF : (j + 1) * LEAF]) * scale
            if j == i:
                tile = tile + jnp.where(sub == lane, REG, 0.0)
            out_ref[own, j * LEAF : (j + 1) * LEAF] = tile
            if j < i:
                out_ref[pl.ds(j * LEAF, LEAF), i * LEAF : (i + 1) * LEAF] = jnp.transpose(tile)
    panel_ref[...] = jnp.zeros((width, LEAF), F32)
    strip_ref[...] = out_ref[0:LEAF, :]
    eliminate(out_ref, panel_ref, strip_ref, 0, steps)


def finish_kernel(in_ref, panel_in_ref, strip_in_ref, out_ref, panel_ref, strip_ref, *, first, last):
    out_ref[...] = in_ref[...]
    panel_ref[...] = panel_in_ref[...]
    strip_ref[...] = strip_in_ref[...]
    eliminate(out_ref, panel_ref, strip_ref, first, last)
    update(out_ref, panel_ref, strip_ref, block(last - 1))


def regress_kernel(tower_ref, inv_ref, own_ref, other_ref, sums_ref, osums_ref, hi_ref, lo_ref):
    width = inv_ref.shape[0]
    half = width // 2
    scale = 1.0 / (sums_ref[1:2, :] - 1.0)

    def centred(ref, at, left_sums, right_mean):
        column = jnp.transpose(jnp.broadcast_to(left_sums[:, at : at + LEAF], (LEAF, LEAF)))
        column = jnp.concatenate([column] * (width // LEAF), axis=1)
        return (ref[pl.ds(at % half, LEAF), :] - column * right_mean) * scale

    def cut(low_ref, high_ref, left_sums, right_mean):
        for i in range(0, width, LEAF):
            ref = low_ref if i < half else high_ref
            hi, lo = split(centred(ref, i, left_sums, right_mean))
            hi_ref[i : i + LEAF, :] = hi
            lo_ref[i : i + LEAF, :] = lo

    def product(left, right):
        (ah, al), (bh, bl) = left, right
        return dot(ah, bh) + (dot(ah, bl) + dot(al, bh))

    @pl.when(tower_ref[0] == 0)
    def _():
        cut(own_ref, other_ref, sums_ref[0:1, :], osums_ref[2:3, :])
        right = hi_ref[...], lo_ref[...]
        for i in range(0, width, 256):
            hi, lo = split(product(split(inv_ref[i : i + 256, :]), right))
            hi_ref[i : i + 256, :] = hi
            lo_ref[i : i + 256, :] = lo

    @pl.when(tower_ref[0] != 0)
    def _():
        cut(other_ref, own_ref, osums_ref[0:1, :], sums_ref[2:3, :])
        right = split(inv_ref[...])
        for i in range(0, width, 256):
            hi, lo = split(product((hi_ref[i : i + 256, :], lo_ref[i : i + 256, :]), right))
            hi_ref[i : i + 256, :] = hi
            lo_ref[i : i + 256, :] = lo


def residual_kernel(tower_ref, count_ref, own_ref, other_ref, sums_ref, osums_ref, hi_ref, lo_ref, out_ref):
    rows, width = own_ref.shape

    def fit(dims):
        mean_hi, mean_lo = split(jnp.broadcast_to(sums_ref[2:3, :], (8, width)))
        shift = dot(mean_hi, hi_ref[...], dims) + (
            dot(mean_hi, lo_ref[...], dims) + dot(mean_lo, hi_ref[...], dims)
        )
        shift = shift[0:1, :] - osums_ref[2:3, :]
        for i in range(0, rows, 256):
            x = own_ref[i : i + 256, :]
            made = dot(x, hi_ref[...], dims) + dot(x, lo_ref[...], dims)
            res = other_ref[i : i + 256, :].astype(F32) - made + shift
            valid = i + lax.broadcasted_iota(jnp.int32, (256, width), 0) < count_ref[0]
            out_ref[i : i + 256, :] = jnp.where(valid, res, 0.0).astype(BF16)

    @pl.when(tower_ref[0] == 0)
    def _():
        fit(((1,), (0,)))

    @pl.when(tower_ref[0] != 0)
    def _():
        fit(((1,), (1,)))


def gradient_kernel(tower_ref, res_ref, inv_ref, hi_ref, lo_ref, ohi_ref, olo_ref, out_ref, corr_ref):
    rows, width = res_ref.shape

    def rows_back(dims):
        ih, il = split(inv_ref[...])
        for i in range(0, rows, 256):
            r = res_ref[i : i + 256, :]
            bh, bl = split(dot(r, ohi_ref[...], dims) + dot(r, olo_ref[...], dims))
            out_ref[i : i + 256, :] = (dot(bh, ih) + (dot(bh, il) + dot(bl, ih))).astype(BF16)

    @pl.when(tower_ref[0] == 0)
    def _():
        rows_back(((1,), (1,)))

    @pl.when(tower_ref[0] != 0)
    def _():
        rows_back(((1,), (0,)))

    acc = jnp.zeros((32, width), F32)
    for i in range(0, width, 32):
        here = pl.ds(i, 32)
        mine = hi_ref[here, :].astype(F32) + lo_ref[here, :].astype(F32)
        theirs = ohi_ref[here, :].astype(F32) + olo_ref[here, :].astype(F32)
        acc = acc + mine * theirs
    corr_ref[...] = jnp.broadcast_to(jnp.sum(acc), (8, LEAF)) / width


def on_device(embeds, counts):
    own = embeds[0]
    rows, width = own.shape
    blocks = width // LEAF
    half = width // 2
    subs, depths = lax.axis_size("sub"), lax.axis_size("depth")
    sub_index = index_of("sub")
    tower = index_of("tower")
    swap = bit_perm(lax.axis_size("tower"), 1)
    other = lax.ppermute(own, "tower", swap)
    wide = (blocks + 1) * LEAF

    gram = call(
        gram_kernel,
        (full((half // subs, wide), F32),) * subs,
        2,
        1,
        [pltpu.VMEM((rows, width), BF16), pltpu.VMEM((half, wide), F32)],
    )(sub_index, counts, own)
    gram_got = swap_all(gram, "sub")
    cross = call(
        cross_kernel, (full((half // subs, width), F32),) * subs, 3, 2, [pltpu.VMEM((half, width), F32)]
    )(sub_index, tower, counts, own, other)

    direct = half // subs % (8 * depths) == 0
    if direct:
        gram_part = sum_split(gram[0], gram_got, "depth")
        gram_part, cross = tie(gram_part, list(cross))
        gram_sum = total(gram_part[0], swap_all(gram_part, "depth"))
        cross_part = sum_split(cross[0], swap_all(cross, "sub"), "depth")
        gram_strip = join(spread(gram_sum, "depth"), "depth")
        gram_strip, cross_part = tie(gram_strip, cross_part)
        gram_all = spread(gram_strip, "sub")
        cross_sum = total(cross_part[0], swap_all(cross_part, "depth"))
        cross_sum, gram_all = tie(cross_sum, gram_all)
        cross_got = spread(cross_sum, "depth")
    else:
        gram_all = spread(lax.psum(total(gram[0], gram_got), "depth"), "sub")
        cross_sum = lax.psum(total(cross[0], swap_all(cross, "sub")), "depth")

    steps = 2
    square = full((width, width), F32)
    panel, strip = full((width, LEAF), F32), full((LEAF, width), F32)
    state, sums, *pending = call(
        functools.partial(begin_kernel, steps=steps),
        (square, full((8, width), F32), panel, strip),
        1,
        subs,
        [pltpu.VMEM((half, wide), F32)],
    )(sub_index, *gram_all)
    cross_strip = join(cross_got, "depth") if direct else cross_sum
    cross_strip, (state, pending) = tie(cross_strip, (state, pending))
    other_sums = lax.ppermute(sums, "tower", swap)
    cross_all = spread(cross_strip, "sub")
    inv = call(
        functools.partial(finish_kernel, first=steps, last=blocks),
        square,
        0,
        3,
        [pltpu.VMEM((width, LEAF), F32), pltpu.VMEM((LEAF, width), F32)],
    )(state, *pending)
    my_half = join(cross_all, "sub")
    their_half = lax.ppermute(my_half, "tower", swap)

    parts = (full((width, width), BF16),) * 2
    hi, lo = call(regress_kernel, parts, 1, 5)(tower, inv, my_half, their_half, sums, other_sums)
    other_hi = lax.ppermute(hi, "tower", swap)
    other_lo = lax.ppermute(lo, "tower", swap)
    res = call(residual_kernel, full((rows, width), BF16), 2, 6)(
        tower, counts, own, other, sums, other_sums, hi, lo
    )
    grad, corr = call(gradient_kernel, (full((rows, width), BF16), full((8, LEAF), F32)), 1, 6)(
        tower, res, inv, hi, lo, other_hi, other_lo
    )
    return grad[None], corr[0, 0]


def solution(mesh):
    placed = (P("tower", ("depth", "sub"), None), P(("depth", "sub")))
    return jax.shard_map(
        on_device,
        mesh=mesh,
        in_specs=placed,
        out_specs=(P("tower", ("depth", "sub"), None), P()),
        check_vma=False,
    )
```

```python
import functools

import jax
import jax.numpy as jnp
from jax import lax
from jax.experimental import pallas as pl
from jax.experimental.pallas import tpu as pltpu
from jax.sharding import PartitionSpec as P

REG = 0.001
LEAF = 128
F32 = jnp.float32
BF16 = jnp.bfloat16
VMEM_LIMIT = 24 << 20


def shift_perm(size, apart):
    return [(source, (source + apart) % size) for source in range(size)]


def bit_perm(size, mask):
    return [(source, source ^ mask) for source in range(size)]


def halving_masks(size):
    return [1 << b for b in range(size.bit_length() - 1)]


def swap_all(pieces, axis):
    size = lax.axis_size(axis)
    return [lax.ppermute(pieces[d], axis, bit_perm(size, d)) for d in range(1, size)]


def spread(piece, axis):
    size = lax.axis_size(axis)
    return [piece] + [lax.ppermute(piece, axis, bit_perm(size, d)) for d in range(1, size)]


def index_of(axis):
    return lax.axis_index(axis).astype(jnp.int32).reshape(1)


def tie(first, then):
    return lax.optimization_barrier((first, then))


def sum_split(own, got, axis):
    size = lax.axis_size(axis)
    rows, wide = own.shape
    part = full((rows // size, wide), F32)
    return list(call(split_kernel, (part,) * size, 1, 1 + len(got))(index_of(axis), own, *got))


def total(own, got):
    return call(total_kernel, full(own.shape, F32), 0, 1 + len(got))(own, *got)


def join(pieces, axis):
    rows, wide = pieces[0].shape
    whole = full((rows * len(pieces), wide), F32)
    return call(join_kernel, whole, 1, len(pieces))(index_of(axis), *pieces)


def split(x):
    hi = x.astype(BF16)
    return hi, (x - hi.astype(F32)).astype(BF16)


def dot(a, b, dims=((1,), (0,))):
    return lax.dot_general(a, b, (dims, ((), ())), preferred_element_type=F32)


def dot3(a, b):
    (ah, al), (bh, bl) = split(a), split(b)
    return dot(ah, bh) + (dot(ah, bl) + dot(al, bh))


def full(shape, dtype):
    return jax.ShapeDtypeStruct(shape, dtype)


def smem():
    return pl.BlockSpec(memory_space=pltpu.SMEM)


def vmem():
    return pl.BlockSpec(memory_space=pltpu.VMEM)


def kept(shape, dtype):
    return pltpu.VMEM(shape, dtype)


def call(kernel, out_shape, n_smem, n_vmem, scratch=()):
    return pl.pallas_call(
        kernel,
        out_shape=out_shape,
        in_specs=[smem()] * n_smem + [vmem()] * n_vmem,
        out_specs=jax.tree.map(lambda _: vmem(), out_shape),
        scratch_shapes=list(scratch),
        compiler_params=pltpu.CompilerParams(vmem_limit_bytes=VMEM_LIMIT),
    )


def split_kernel(me_ref, *refs):
    outs = [ref for ref in refs if ref.shape[0] != refs[0].shape[0]]
    ins = refs[: len(refs) - len(outs)]
    rows = outs[0].shape[0]
    for d, out_ref in enumerate(outs):
        here = pl.ds(pl.multiple_of((me_ref[0] ^ d) * rows, rows), rows)
        acc = ins[0][here, :]
        for ref in ins[1:]:
            acc = acc + ref[here, :]
        out_ref[...] = acc


def total_kernel(*refs):
    acc = refs[0][...]
    for ref in refs[1:-1]:
        acc = acc + ref[...]
    refs[-1][...] = acc


def join_kernel(me_ref, *refs):
    rows = refs[0].shape[0]
    for d, ref in enumerate(refs[:-1]):
        refs[-1][pl.ds(pl.multiple_of((me_ref[0] ^ d) * rows, rows), rows), :] = ref[...]


def deal(me, source_ref, outs):
    rows = outs[0].shape[0]
    for d, out_ref in enumerate(outs):
        out_ref[...] = source_ref[pl.ds(pl.multiple_of((me ^ d) * rows, rows), rows), :]


def gram_kernel(me_ref, count_ref, x_ref, *refs):
    outs, masked_ref, out_ref = refs[:-2], refs[-2], refs[-1]
    rows, width = x_ref.shape
    blocks = width // LEAF
    count = count_ref[0]
    valid = lax.broadcasted_iota(jnp.int32, (rows, LEAF), 0) < count
    for j in range(blocks):
        cols = pl.ds(j * LEAF, LEAF)
        masked_ref[:, cols] = jnp.where(valid, x_ref[:, cols].astype(F32), 0.0).astype(BF16)
    sums = dot(jnp.ones((8, rows), BF16), masked_ref[...])
    sub = lax.broadcasted_iota(jnp.int32, (LEAF, LEAF), 0)
    lane = lax.broadcasted_iota(jnp.int32, (LEAF, LEAF), 1)
    for i in range(blocks):
        wide = (i + 1) * LEAF
        strip = dot(masked_ref[:, i * LEAF : wide], masked_ref[:, :wide], ((0,), (0,)))
        tile = strip[:, i * LEAF :]
        mine = sums[0:1, i * LEAF : wide]
        tile = jnp.where((sub == 0) & (lane > 0), mine, tile)
        last = lane == LEAF - 1
        tile = jnp.where((sub == 1) & last, mine[:, 0:1], tile)
        tile = jnp.where((sub == 2) & last, count.astype(F32), tile)
        if i >= blocks // 2:
            at, row = 0, blocks - 1 - i
        else:
            at, row = (blocks - i) * LEAF, i
        here = pl.ds(row * LEAF, LEAF)
        if i:
            out_ref[here, at : at + i * LEAF] = strip[:, : i * LEAF]
        out_ref[here, at + i * LEAF : at + wide] = tile
    deal(me_ref[0], out_ref, outs)


def cross_kernel(me_ref, tower_ref, count_ref, own_ref, other_ref, *refs):
    outs, out_ref = refs[:-1], refs[-1]
    rows, width = own_ref.shape
    half = width // 2
    valid = lax.broadcasted_iota(jnp.int32, (rows, half), 0) < count_ref[0]

    def part(left_ref, right_ref, first):
        left = left_ref[:, first : first + half]
        left = jnp.where(valid, left.astype(F32), 0.0).astype(BF16)
        out_ref[...] = dot(left, right_ref[...], ((0,), (0,)))

    @pl.when(tower_ref[0] == 0)
    def _():
        part(own_ref, other_ref, 0)

    @pl.when(tower_ref[0] != 0)
    def _():
        part(other_ref, own_ref, half)

    deal(me_ref[0], out_ref, outs)


def inverse_two(a, b, d):
    scale = 1.0 / (a * d - b * b)
    return d * scale, -b * scale, a * scale


def inverse_four(p):
    e00, e01, e11 = inverse_two(p[0][0], p[0][1], p[1][1])
    b00, b01, b10, b11 = p[0][2], p[0][3], p[1][2], p[1][3]
    f00, f01 = e00 * b00 + e01 * b10, e00 * b01 + e01 * b11
    f10, f11 = e01 * b00 + e11 * b10, e01 * b01 + e11 * b11
    g00, g01, g11 = inverse_two(
        p[2][2] - (b00 * f00 + b10 * f10),
        p[2][3] - (b00 * f01 + b10 * f11),
        p[3][3] - (b01 * f01 + b11 * f11),
    )
    h00, h01 = -(f00 * g00 + f01 * g01), -(f00 * g01 + f01 * g11)
    h10, h11 = -(f10 * g00 + f11 * g01), -(f10 * g01 + f11 * g11)
    q00 = e00 - (h00 * f00 + h01 * f01)
    q01 = e01 - (h00 * f10 + h01 * f11)
    q11 = e11 - (h10 * f10 + h11 * f11)
    return [
        [q00, q01, h00, h01],
        [q01, q11, h10, h11],
        [h00, h10, g00, g01],
        [h01, h11, g01, g11],
    ]


PIVOT = 4


def leaf_inverse(block):
    size = block.shape[0]
    tile = (8, size)
    tiles = [block[8 * i : 8 * i + 8, :] for i in range(size // 8)]
    lane = lax.broadcasted_iota(jnp.int32, tile, 1)
    sub = lax.broadcasted_iota(jnp.int32, tile, 0)
    span = range(PIVOT)
    for first in range(0, size, PIVOT):
        home, row = first // 8, first % 8
        rows = [jnp.broadcast_to(tiles[home][row + a : row + a + 1, :], tile) for a in span]
        pivot = [[None] * PIVOT for _ in span]
        for a in span:
            for b in range(a, PIVOT):
                entry = jnp.broadcast_to(rows[a][:, first + b : first + b + 1], tile)
                pivot[a][b] = pivot[b][a] = entry
        cols = [
            [jnp.broadcast_to(t[:, first + b : first + b + 1], tile) for t in tiles] for b in span
        ]
        inv = inverse_four(pivot)
        inside = (lane >= first) & (lane < first + PIVOT)
        rows = [jnp.where(inside, jnp.where(lane == first + a, 1.0, 0.0), rows[a]) for a in span]
        scaled = []
        for a in span:
            acc = inv[a][0] * rows[0]
            for b in range(1, PIVOT):
                acc = acc + inv[a][b] * rows[b]
            scaled.append(acc)
        fresh = []
        for i, old in enumerate(tiles):
            acc = jnp.where(inside, 0.0, old)
            for a in span:
                acc = acc - cols[a][i] * scaled[a]
            if i == home:
                for a in span:
                    acc = jnp.where(sub == row + a, scaled[a], acc)
            fresh.append(acc)
        tiles = fresh
    return jnp.concatenate(tiles, axis=0)


def update(out_ref, panel_ref, strip_ref, prev):
    high, low = split(strip_ref[...])
    for i in range(0, out_ref.shape[0], 256):
        ph, plo = split(panel_ref[i : i + 256, :])
        product = dot(ph, high) + (dot(ph, low) + dot(plo, high))
        out_ref[i : i + 256, :] = out_ref[i : i + 256, :] - product
    out_ref[prev, :] = strip_ref[...]


def block(k):
    return pl.ds(pl.multiple_of(k * LEAF, LEAF), LEAF)


def eliminate(out_ref, panel_ref, strip_ref, first, last):
    width = out_ref.shape[0]
    sub = lax.broadcasted_iota(jnp.int32, (LEAF, LEAF), 0)
    lane = lax.broadcasted_iota(jnp.int32, (LEAF, LEAF), 1)

    def body(k, carry):
        here = block(k)
        inv = leaf_inverse(out_ref[here, here] - dot3(panel_ref[here, :], strip_ref[:, here]))
        update(out_ref, panel_ref, strip_ref, block(jnp.maximum(k - 1, 0)))
        panel_ref[...] = out_ref[:, here]
        out_ref[:, here] = jnp.zeros((width, LEAF), F32)
        out_ref[here, here] = jnp.where(sub == lane, 1.0, 0.0)
        strip_ref[...] = dot3(inv, out_ref[here, :])
        panel_ref[here, :] = jnp.zeros((LEAF, LEAF), F32)
        return carry

    lax.fori_loop(first, last, body, 0)


def begin_kernel(me_ref, *refs, steps):
    ins, (out_ref, sums_ref, panel_ref, strip_ref, packed_ref) = refs[:-5], refs[-5:]
    width = out_ref.shape[0]
    blocks = width // LEAF
    sub = lax.broadcasted_iota(jnp.int32, (LEAF, LEAF), 0)
    lane = lax.broadcasted_iota(jnp.int32, (LEAF, LEAF), 1)
    rows = ins[0].shape[0]
    for d, ref in enumerate(ins):
        packed_ref[pl.ds(pl.multiple_of((me_ref[0] ^ d) * rows, rows), rows), :] = ref[...]

    def packed(i):
        if i >= blocks // 2:
            return pl.ds((blocks - 1 - i) * LEAF, LEAF), 0
        return pl.ds(i * LEAF, LEAF), (blocks - i) * LEAF

    for i in range(blocks):
        here, at = packed(i)
        tile = packed_ref[here, at + i * LEAF : at + (i + 1) * LEAF]
        first = tile[1:2, LEAF - 1 : LEAF]
        mine = jnp.where(lane[0:1] == 0, first, tile[0:1, :])
        sums_ref[0:1, i * LEAF : (i + 1) * LEAF] = mine
        if i == 0:
            count = jnp.broadcast_to(tile[2:3, LEAF - 1 : LEAF], (1, LEAF))
    wide_count = jnp.concatenate([count] * blocks, axis=1)
    sums_ref[1:2, :] = wide_count
    sums_ref[2:3, :] = sums_ref[0:1, :] / wide_count
    sums_ref[3:8, :] = jnp.zeros((5, width), F32)
    scale = 1.0 / (count - 1.0)
    means = sums_ref[2:3, :]
    for i in range(blocks):
        here, at = packed(i)
        own = pl.ds(i * LEAF, LEAF)
        column = jnp.transpose(jnp.broadcast_to(sums_ref[0:1, i * LEAF : (i + 1) * LEAF], (LEAF, LEAF)))
        for j in range(i + 1):
            tile = packed_ref[here, at + j * LEAF : at + (j + 1) * LEAF]
            if j == i:
                tile = jnp.where(sub >= lane, tile, jnp.transpose(tile))
            tile = (tile - column * means[:, j * LEAF : (j + 1) * LEAF]) * scale
            if j == i:
                tile = tile + jnp.where(sub == lane, REG, 0.0)
            out_ref[own, j * LEAF : (j + 1) * LEAF] = tile
            if j < i:
                out_ref[pl.ds(j * LEAF, LEAF), i * LEAF : (i + 1) * LEAF] = jnp.transpose(tile)
    panel_ref[...] = jnp.zeros((width, LEAF), F32)
    strip_ref[...] = out_ref[0:LEAF, :]
    eliminate(out_ref, panel_ref, strip_ref, 0, steps)


def finish_kernel(in_ref, panel_in_ref, strip_in_ref, out_ref, panel_ref, strip_ref, *, first, last):
    out_ref[...] = in_ref[...]
    panel_ref[...] = panel_in_ref[...]
    strip_ref[...] = strip_in_ref[...]
    eliminate(out_ref, panel_ref, strip_ref, first, last)
    update(out_ref, panel_ref, strip_ref, block(last - 1))


def regress_kernel(tower_ref, inv_ref, own_ref, other_ref, sums_ref, osums_ref, hi_ref, lo_ref):
    width = inv_ref.shape[0]
    half = width // 2
    scale = 1.0 / (sums_ref[1:2, :] - 1.0)

    def centred(ref, at, left_sums, right_mean):
        column = jnp.transpose(jnp.broadcast_to(left_sums[:, at : at + LEAF], (LEAF, LEAF)))
        column = jnp.concatenate([column] * (width // LEAF), axis=1)
        return (ref[pl.ds(at % half, LEAF), :] - column * right_mean) * scale

    def cut(low_ref, high_ref, left_sums, right_mean):
        for i in range(0, width, LEAF):
            ref = low_ref if i < half else high_ref
            hi, lo = split(centred(ref, i, left_sums, right_mean))
            hi_ref[i : i + LEAF, :] = hi
            lo_ref[i : i + LEAF, :] = lo

    def product(left, right):
        (ah, al), (bh, bl) = left, right
        return dot(ah, bh) + (dot(ah, bl) + dot(al, bh))

    @pl.when(tower_ref[0] == 0)
    def _():
        cut(own_ref, other_ref, sums_ref[0:1, :], osums_ref[2:3, :])
        right = hi_ref[...], lo_ref[...]
        for i in range(0, width, 256):
            hi, lo = split(product(split(inv_ref[i : i + 256, :]), right))
            hi_ref[i : i + 256, :] = hi
            lo_ref[i : i + 256, :] = lo

    @pl.when(tower_ref[0] != 0)
    def _():
        cut(other_ref, own_ref, osums_ref[0:1, :], sums_ref[2:3, :])
        right = split(inv_ref[...])
        for i in range(0, width, 256):
            hi, lo = split(product((hi_ref[i : i + 256, :], lo_ref[i : i + 256, :]), right))
            hi_ref[i : i + 256, :] = hi
            lo_ref[i : i + 256, :] = lo


def residual_kernel(tower_ref, count_ref, own_ref, other_ref, sums_ref, osums_ref, hi_ref, lo_ref, out_ref):
    rows, width = own_ref.shape

    def fit(dims):
        mean_hi, mean_lo = split(jnp.broadcast_to(sums_ref[2:3, :], (8, width)))
        shift = dot(mean_hi, hi_ref[...], dims) + (
            dot(mean_hi, lo_ref[...], dims) + dot(mean_lo, hi_ref[...], dims)
        )
        shift = shift[0:1, :] - osums_ref[2:3, :]
        for i in range(0, rows, 256):
            x = own_ref[i : i + 256, :]
            made = dot(x, hi_ref[...], dims) + dot(x, lo_ref[...], dims)
            res = other_ref[i : i + 256, :].astype(F32) - made + shift
            valid = i + lax.broadcasted_iota(jnp.int32, (256, width), 0) < count_ref[0]
            out_ref[i : i + 256, :] = jnp.where(valid, res, 0.0).astype(BF16)

    @pl.when(tower_ref[0] == 0)
    def _():
        fit(((1,), (0,)))

    @pl.when(tower_ref[0] != 0)
    def _():
        fit(((1,), (1,)))


def gradient_kernel(tower_ref, res_ref, inv_ref, hi_ref, lo_ref, ohi_ref, olo_ref, out_ref, corr_ref):
    rows, width = res_ref.shape

    def rows_back(dims):
        ih, il = split(inv_ref[...])
        for i in range(0, rows, 256):
            r = res_ref[i : i + 256, :]
            bh, bl = split(dot(r, ohi_ref[...], dims) + dot(r, olo_ref[...], dims))
            out_ref[i : i + 256, :] = (dot(bh, ih) + (dot(bh, il) + dot(bl, ih))).astype(BF16)

    @pl.when(tower_ref[0] == 0)
    def _():
        rows_back(((1,), (1,)))

    @pl.when(tower_ref[0] != 0)
    def _():
        rows_back(((1,), (0,)))

    acc = jnp.zeros((32, width), F32)
    for i in range(0, width, 32):
        here = pl.ds(i, 32)
        mine = hi_ref[here, :].astype(F32) + lo_ref[here, :].astype(F32)
        theirs = ohi_ref[here, :].astype(F32) + olo_ref[here, :].astype(F32)
        acc = acc + mine * theirs
    corr_ref[...] = jnp.broadcast_to(jnp.sum(acc), (8, LEAF)) / width


def on_device(embeds, counts):
    own = embeds[0]
    rows, width = own.shape
    blocks = width // LEAF
    half = width // 2
    subs, depths = lax.axis_size("sub"), lax.axis_size("depth")
    sub_index = index_of("sub")
    tower = index_of("tower")
    swap = bit_perm(lax.axis_size("tower"), 1)
    other = lax.ppermute(own, "tower", swap)
    wide = (blocks + 1) * LEAF

    gram = call(
        gram_kernel,
        (full((half // subs, wide), F32),) * subs,
        2,
        1,
        [pltpu.VMEM((rows, width), BF16), pltpu.VMEM((half, wide), F32)],
    )(sub_index, counts, own)
    gram_got = swap_all(gram, "sub")
    cross = call(
        cross_kernel, (full((half // subs, width), F32),) * subs, 3, 2, [pltpu.VMEM((half, width), F32)]
    )(sub_index, tower, counts, own, other)
    cross, gram_got = tie(list(cross), gram_got)

    direct = half // subs % (8 * depths) == 0
    if direct:
        gram_part = sum_split(gram[0], gram_got, "depth")
        gram_part, cross = tie(gram_part, list(cross))
        gram_sum = total(gram_part[0], swap_all(gram_part, "depth"))
        cross_part = sum_split(cross[0], swap_all(cross, "sub"), "depth")
        gram_strip = join(spread(gram_sum, "depth"), "depth")
        gram_strip, cross_part = tie(gram_strip, cross_part)
        gram_all = spread(gram_strip, "sub")
        cross_sum = total(cross_part[0], swap_all(cross_part, "depth"))
        cross_sum, gram_all = tie(cross_sum, gram_all)
        cross_got = spread(cross_sum, "depth")
    else:
        gram_all = spread(lax.psum(total(gram[0], gram_got), "depth"), "sub")
        cross_sum = lax.psum(total(cross[0], swap_all(cross, "sub")), "depth")

    steps = 2
    square = kept((width, width), F32)
    panel, strip = kept((width, LEAF), F32), kept((LEAF, width), F32)
    state, sums, *pending = call(
        functools.partial(begin_kernel, steps=steps),
        (square, full((8, width), F32), panel, strip),
        1,
        subs,
        [pltpu.VMEM((half, wide), F32)],
    )(sub_index, *gram_all)
    cross_strip = join(cross_got, "depth") if direct else cross_sum
    cross_strip, (state, pending) = tie(cross_strip, (state, pending))
    other_sums = lax.ppermute(sums, "tower", swap)
    cross_all = spread(cross_strip, "sub")
    inv = call(
        functools.partial(finish_kernel, first=steps, last=blocks),
        square,
        0,
        3,
        [pltpu.VMEM((width, LEAF), F32), pltpu.VMEM((LEAF, width), F32)],
    )(state, *pending)
    my_half, inv = tie(join(cross_all, "sub"), inv)
    their_half = lax.ppermute(my_half, "tower", swap)

    parts = (full((width, width), BF16),) * 2
    hi, lo = call(regress_kernel, parts, 1, 5)(tower, inv, my_half, their_half, sums, other_sums)
    other_hi = lax.ppermute(hi, "tower", swap)
    other_lo = lax.ppermute(lo, "tower", swap)
    res = call(residual_kernel, kept((rows, width), BF16), 2, 6)(
        tower, counts, own, other, sums, other_sums, hi, lo
    )
    grad, corr = call(gradient_kernel, (full((rows, width), BF16), full((8, LEAF), F32)), 1, 6)(
        tower, res, inv, hi, lo, other_hi, other_lo
    )
    return grad[None], corr[0, 0]


def solution(mesh):
    placed = (P("tower", ("depth", "sub"), None), P(("depth", "sub")))
    return jax.shard_map(
        on_device,
        mesh=mesh,
        in_specs=placed,
        out_specs=(P("tower", ("depth", "sub"), None), P()),
        check_vma=False,
    )
```

```python
import functools

import jax
import jax.numpy as jnp
from jax import lax
from jax.experimental import pallas as pl
from jax.experimental.pallas import tpu as pltpu
from jax.sharding import PartitionSpec as P

REG = 0.001
LEAF = 128
F32 = jnp.float32
BF16 = jnp.bfloat16
VMEM_LIMIT = 24 << 20


def shift_perm(size, apart):
    return [(source, (source + apart) % size) for source in range(size)]


def bit_perm(size, mask):
    return [(source, source ^ mask) for source in range(size)]


def halving_masks(size):
    return [1 << b for b in range(size.bit_length() - 1)]


def swap_all(pieces, axis):
    size = lax.axis_size(axis)
    return [lax.ppermute(pieces[d], axis, bit_perm(size, d)) for d in range(1, size)]


def spread(piece, axis):
    size = lax.axis_size(axis)
    return [piece] + [lax.ppermute(piece, axis, bit_perm(size, d)) for d in range(1, size)]


def index_of(axis):
    return lax.axis_index(axis).astype(jnp.int32).reshape(1)


def tie(first, then):
    return lax.optimization_barrier((first, then))


def sum_split(own, got, axis):
    size = lax.axis_size(axis)
    rows, wide = own.shape
    part = full((rows // size, wide), F32)
    return list(call(split_kernel, (part,) * size, 1, 1 + len(got))(index_of(axis), own, *got))


def total(own, got):
    return call(total_kernel, full(own.shape, F32), 0, 1 + len(got))(own, *got)


def join(pieces, axis):
    rows, wide = pieces[0].shape
    whole = full((rows * len(pieces), wide), F32)
    return call(join_kernel, whole, 1, len(pieces))(index_of(axis), *pieces)


def split(x):
    hi = x.astype(BF16)
    return hi, (x - hi.astype(F32)).astype(BF16)


def dot(a, b, dims=((1,), (0,))):
    return lax.dot_general(a, b, (dims, ((), ())), preferred_element_type=F32)


def wide_left(a):
    hi, lo = split(a)
    return jnp.concatenate([hi, hi, lo], axis=1)


def wide_right(b):
    hi, lo = split(b)
    return jnp.concatenate([hi, lo, hi], axis=0)


def dot3(a, b):
    return dot(wide_left(a), wide_right(b))


def full(shape, dtype):
    return jax.ShapeDtypeStruct(shape, dtype)


def smem():
    return pl.BlockSpec(memory_space=pltpu.SMEM)


def vmem():
    return pl.BlockSpec(memory_space=pltpu.VMEM)


def kept(shape, dtype):
    return pltpu.VMEM(shape, dtype)


def call(kernel, out_shape, n_smem, n_vmem, scratch=()):
    return pl.pallas_call(
        kernel,
        out_shape=out_shape,
        in_specs=[smem()] * n_smem + [vmem()] * n_vmem,
        out_specs=jax.tree.map(lambda _: vmem(), out_shape),
        scratch_shapes=list(scratch),
        compiler_params=pltpu.CompilerParams(vmem_limit_bytes=VMEM_LIMIT),
    )


def split_kernel(me_ref, *refs):
    outs = [ref for ref in refs if ref.shape[0] != refs[0].shape[0]]
    ins = refs[: len(refs) - len(outs)]
    rows = outs[0].shape[0]
    for d, out_ref in enumerate(outs):
        here = pl.ds(pl.multiple_of((me_ref[0] ^ d) * rows, rows), rows)
        acc = ins[0][here, :]
        for ref in ins[1:]:
            acc = acc + ref[here, :]
        out_ref[...] = acc


def total_kernel(*refs):
    acc = refs[0][...]
    for ref in refs[1:-1]:
        acc = acc + ref[...]
    refs[-1][...] = acc


def join_kernel(me_ref, *refs):
    rows = refs[0].shape[0]
    for d, ref in enumerate(refs[:-1]):
        refs[-1][pl.ds(pl.multiple_of((me_ref[0] ^ d) * rows, rows), rows), :] = ref[...]


def deal(me, source_ref, outs):
    rows = outs[0].shape[0]
    for d, out_ref in enumerate(outs):
        out_ref[...] = source_ref[pl.ds(pl.multiple_of((me ^ d) * rows, rows), rows), :]


def gram_kernel(me_ref, count_ref, x_ref, *refs):
    outs, masked_ref, out_ref = refs[:-2], refs[-2], refs[-1]
    rows, width = x_ref.shape
    blocks = width // LEAF
    count = count_ref[0]
    valid = lax.broadcasted_iota(jnp.int32, (rows, LEAF), 0) < count
    for j in range(blocks):
        cols = pl.ds(j * LEAF, LEAF)
        masked_ref[:, cols] = jnp.where(valid, x_ref[:, cols].astype(F32), 0.0).astype(BF16)
    sums = dot(jnp.ones((8, rows), BF16), masked_ref[...])
    sub = lax.broadcasted_iota(jnp.int32, (LEAF, LEAF), 0)
    lane = lax.broadcasted_iota(jnp.int32, (LEAF, LEAF), 1)
    for i in range(blocks):
        wide = (i + 1) * LEAF
        strip = dot(masked_ref[:, i * LEAF : wide], masked_ref[:, :wide], ((0,), (0,)))
        tile = strip[:, i * LEAF :]
        mine = sums[0:1, i * LEAF : wide]
        tile = jnp.where((sub == 0) & (lane > 0), mine, tile)
        last = lane == LEAF - 1
        tile = jnp.where((sub == 1) & last, mine[:, 0:1], tile)
        tile = jnp.where((sub == 2) & last, count.astype(F32), tile)
        if i >= blocks // 2:
            at, row = 0, blocks - 1 - i
        else:
            at, row = (blocks - i) * LEAF, i
        here = pl.ds(row * LEAF, LEAF)
        if i:
            out_ref[here, at : at + i * LEAF] = strip[:, : i * LEAF]
        out_ref[here, at + i * LEAF : at + wide] = tile
    deal(me_ref[0], out_ref, outs)


def cross_kernel(me_ref, tower_ref, count_ref, own_ref, other_ref, *refs):
    outs, out_ref = refs[:-1], refs[-1]
    rows, width = own_ref.shape
    half = width // 2
    valid = lax.broadcasted_iota(jnp.int32, (rows, half), 0) < count_ref[0]

    def part(left_ref, right_ref, first):
        left = left_ref[:, first : first + half]
        left = jnp.where(valid, left.astype(F32), 0.0).astype(BF16)
        out_ref[...] = dot(left, right_ref[...], ((0,), (0,)))

    @pl.when(tower_ref[0] == 0)
    def _():
        part(own_ref, other_ref, 0)

    @pl.when(tower_ref[0] != 0)
    def _():
        part(other_ref, own_ref, half)

    deal(me_ref[0], out_ref, outs)


def inverse_two(a, b, d):
    scale = 1.0 / (a * d - b * b)
    return d * scale, -b * scale, a * scale


def inverse_four(p):
    e00, e01, e11 = inverse_two(p[0][0], p[0][1], p[1][1])
    b00, b01, b10, b11 = p[0][2], p[0][3], p[1][2], p[1][3]
    f00, f01 = e00 * b00 + e01 * b10, e00 * b01 + e01 * b11
    f10, f11 = e01 * b00 + e11 * b10, e01 * b01 + e11 * b11
    g00, g01, g11 = inverse_two(
        p[2][2] - (b00 * f00 + b10 * f10),
        p[2][3] - (b00 * f01 + b10 * f11),
        p[3][3] - (b01 * f01 + b11 * f11),
    )
    h00, h01 = -(f00 * g00 + f01 * g01), -(f00 * g01 + f01 * g11)
    h10, h11 = -(f10 * g00 + f11 * g01), -(f10 * g01 + f11 * g11)
    q00 = e00 - (h00 * f00 + h01 * f01)
    q01 = e01 - (h00 * f10 + h01 * f11)
    q11 = e11 - (h10 * f10 + h11 * f11)
    return [
        [q00, q01, h00, h01],
        [q01, q11, h10, h11],
        [h00, h10, g00, g01],
        [h01, h11, g01, g11],
    ]


PIVOT = 4


def leaf_inverse(block):
    size = block.shape[0]
    tile = (8, size)
    tiles = [block[8 * i : 8 * i + 8, :] for i in range(size // 8)]
    lane = lax.broadcasted_iota(jnp.int32, tile, 1)
    sub = lax.broadcasted_iota(jnp.int32, tile, 0)
    span = range(PIVOT)
    for first in range(0, size, PIVOT):
        home, row = first // 8, first % 8
        rows = [jnp.broadcast_to(tiles[home][row + a : row + a + 1, :], tile) for a in span]
        pivot = [[None] * PIVOT for _ in span]
        for a in span:
            for b in range(a, PIVOT):
                entry = jnp.broadcast_to(rows[a][:, first + b : first + b + 1], tile)
                pivot[a][b] = pivot[b][a] = entry
        cols = [
            [jnp.broadcast_to(t[:, first + b : first + b + 1], tile) for t in tiles] for b in span
        ]
        inv = inverse_four(pivot)
        inside = (lane >= first) & (lane < first + PIVOT)
        rows = [jnp.where(inside, jnp.where(lane == first + a, 1.0, 0.0), rows[a]) for a in span]
        scaled = []
        for a in span:
            acc = inv[a][0] * rows[0]
            for b in range(1, PIVOT):
                acc = acc + inv[a][b] * rows[b]
            scaled.append(acc)
        fresh = []
        for i, old in enumerate(tiles):
            acc = jnp.where(inside, 0.0, old)
            for a in span:
                acc = acc - cols[a][i] * scaled[a]
            if i == home:
                for a in span:
                    acc = jnp.where(sub == row + a, scaled[a], acc)
            fresh.append(acc)
        tiles = fresh
    return jnp.concatenate(tiles, axis=0)


def block(k):
    return pl.ds(pl.multiple_of(k * LEAF, LEAF), LEAF)


def apply_pivot(out_ref, pivot, panel_ref, strip_ref, k, live):
    width = out_ref.shape[0]
    here = block(k)
    sub = lax.broadcasted_iota(jnp.int32, (LEAF, LEAF), 0)
    lane = lax.broadcasted_iota(jnp.int32, (LEAF, LEAF), 1)
    one = jnp.where(sub == lane, 1.0, 0.0)
    old = out_ref[here, :]
    panel_ref[...] = out_ref[:, here] if live is None else jnp.where(live, out_ref[:, here], 0.0)
    out_ref[:, here] = out_ref[:, here] - panel_ref[...]
    out_ref[here, here] = one if live is None else jnp.where(live, one, out_ref[here, here])
    strip = dot3(pivot, out_ref[here, :])
    strip_ref[...] = strip if live is None else jnp.where(live, strip, old)
    panel_ref[here, :] = jnp.zeros((LEAF, LEAF), F32)
    right = wide_right(strip_ref[...])
    for i in range(0, width, 256):
        product = dot(wide_left(panel_ref[i : i + 256, :]), right)
        out_ref[i : i + 256, :] = out_ref[i : i + 256, :] - product
    out_ref[here, :] = strip_ref[...]


def eliminate(out_ref, pivot_ref, panel_ref, strip_ref, first, last):
    blocks = out_ref.shape[0] // LEAF

    def body(ahead, carry):
        live = ahead > 0
        k = jnp.maximum(ahead - 1, 0)
        here, near = block(k), block(ahead)
        pivot = pivot_ref[...]
        side = dot3(out_ref[near, here], dot3(pivot, out_ref[here, near]))
        inv = leaf_inverse(out_ref[near, near] - jnp.where(live, side, 0.0))
        apply_pivot(out_ref, pivot, panel_ref, strip_ref, k, live)
        pivot_ref[...] = inv
        return carry

    lax.fori_loop(first + 1, min(last, blocks - 1) + 1, body, 0)
    if last == blocks:
        apply_pivot(out_ref, pivot_ref[...], panel_ref, strip_ref, blocks - 1, None)


def begin_kernel(me_ref, *refs, steps):
    ins, (out_ref, sums_ref, pivot_ref, packed_ref, panel_ref, strip_ref) = refs[:-6], refs[-6:]
    width = out_ref.shape[0]
    blocks = width // LEAF
    sub = lax.broadcasted_iota(jnp.int32, (LEAF, LEAF), 0)
    lane = lax.broadcasted_iota(jnp.int32, (LEAF, LEAF), 1)
    rows = ins[0].shape[0]
    for d, ref in enumerate(ins):
        packed_ref[pl.ds(pl.multiple_of((me_ref[0] ^ d) * rows, rows), rows), :] = ref[...]

    def packed(i):
        if i >= blocks // 2:
            return pl.ds((blocks - 1 - i) * LEAF, LEAF), 0
        return pl.ds(i * LEAF, LEAF), (blocks - i) * LEAF

    for i in range(blocks):
        here, at = packed(i)
        tile = packed_ref[here, at + i * LEAF : at + (i + 1) * LEAF]
        first = tile[1:2, LEAF - 1 : LEAF]
        mine = jnp.where(lane[0:1] == 0, first, tile[0:1, :])
        sums_ref[0:1, i * LEAF : (i + 1) * LEAF] = mine
        if i == 0:
            count = jnp.broadcast_to(tile[2:3, LEAF - 1 : LEAF], (1, LEAF))
    wide_count = jnp.concatenate([count] * blocks, axis=1)
    sums_ref[1:2, :] = wide_count
    sums_ref[2:3, :] = sums_ref[0:1, :] / wide_count
    sums_ref[3:8, :] = jnp.zeros((5, width), F32)
    scale = 1.0 / (count - 1.0)
    means = sums_ref[2:3, :]
    for i in range(blocks):
        here, at = packed(i)
        own = pl.ds(i * LEAF, LEAF)
        column = jnp.transpose(jnp.broadcast_to(sums_ref[0:1, i * LEAF : (i + 1) * LEAF], (LEAF, LEAF)))
        for j in range(i + 1):
            tile = packed_ref[here, at + j * LEAF : at + (j + 1) * LEAF]
            if j == i:
                tile = jnp.where(sub >= lane, tile, jnp.transpose(tile))
            tile = (tile - column * means[:, j * LEAF : (j + 1) * LEAF]) * scale
            if j == i:
                tile = tile + jnp.where(sub == lane, REG, 0.0)
            out_ref[own, j * LEAF : (j + 1) * LEAF] = tile
            if j < i:
                out_ref[pl.ds(j * LEAF, LEAF), i * LEAF : (i + 1) * LEAF] = jnp.transpose(tile)
    pivot_ref[...] = jnp.zeros((LEAF, LEAF), F32)
    eliminate(out_ref, pivot_ref, panel_ref, strip_ref, -1, steps)


def finish_kernel(in_ref, pivot_in_ref, out_ref, panel_ref, strip_ref, pivot_ref, *, first, last):
    out_ref[...] = in_ref[...]
    pivot_ref[...] = pivot_in_ref[...]
    eliminate(out_ref, pivot_ref, panel_ref, strip_ref, first, last)


def regress_kernel(tower_ref, inv_ref, own_ref, other_ref, sums_ref, osums_ref, hi_ref, lo_ref):
    width = inv_ref.shape[0]
    half = width // 2
    scale = 1.0 / (sums_ref[1:2, :] - 1.0)

    def centred(ref, at, left_sums, right_mean):
        column = jnp.transpose(jnp.broadcast_to(left_sums[:, at : at + LEAF], (LEAF, LEAF)))
        column = jnp.concatenate([column] * (width // LEAF), axis=1)
        return (ref[pl.ds(at % half, LEAF), :] - column * right_mean) * scale

    def cut(low_ref, high_ref, left_sums, right_mean):
        for i in range(0, width, LEAF):
            ref = low_ref if i < half else high_ref
            hi, lo = split(centred(ref, i, left_sums, right_mean))
            hi_ref[i : i + LEAF, :] = hi
            lo_ref[i : i + LEAF, :] = lo

    def product(left, right):
        (ah, al), (bh, bl) = left, right
        return dot(ah, bh) + (dot(ah, bl) + dot(al, bh))

    @pl.when(tower_ref[0] == 0)
    def _():
        cut(own_ref, other_ref, sums_ref[0:1, :], osums_ref[2:3, :])
        right = hi_ref[...], lo_ref[...]
        for i in range(0, width, 256):
            hi, lo = split(product(split(inv_ref[i : i + 256, :]), right))
            hi_ref[i : i + 256, :] = hi
            lo_ref[i : i + 256, :] = lo

    @pl.when(tower_ref[0] != 0)
    def _():
        cut(other_ref, own_ref, osums_ref[0:1, :], sums_ref[2:3, :])
        right = split(inv_ref[...])
        for i in range(0, width, 256):
            hi, lo = split(product((hi_ref[i : i + 256, :], lo_ref[i : i + 256, :]), right))
            hi_ref[i : i + 256, :] = hi
            lo_ref[i : i + 256, :] = lo


def residual_kernel(tower_ref, count_ref, own_ref, other_ref, sums_ref, osums_ref, hi_ref, out_ref):
    rows, width = own_ref.shape

    def fit(dims):
        mean_hi, mean_lo = split(jnp.broadcast_to(sums_ref[2:3, :], (8, width)))
        shift = dot(mean_hi, hi_ref[...], dims) + dot(mean_lo, hi_ref[...], dims)
        shift = shift[0:1, :] - osums_ref[2:3, :]
        for i in range(0, rows, 256):
            x = own_ref[i : i + 256, :]
            made = dot(x, hi_ref[...], dims)
            res = other_ref[i : i + 256, :].astype(F32) - made + shift
            valid = i + lax.broadcasted_iota(jnp.int32, (256, width), 0) < count_ref[0]
            out_ref[i : i + 256, :] = jnp.where(valid, res, 0.0).astype(BF16)

    @pl.when(tower_ref[0] == 0)
    def _():
        fit(((1,), (0,)))

    @pl.when(tower_ref[0] != 0)
    def _():
        fit(((1,), (1,)))


def gradient_kernel(tower_ref, res_ref, inv_ref, hi_ref, lo_ref, ohi_ref, olo_ref, out_ref, corr_ref):
    rows, width = res_ref.shape

    def rows_back(dims):
        ih, il = split(inv_ref[...])
        for i in range(0, rows, 256):
            r = res_ref[i : i + 256, :]
            bh, bl = split(dot(r, ohi_ref[...], dims) + dot(r, olo_ref[...], dims))
            out_ref[i : i + 256, :] = (dot(bh, ih) + (dot(bh, il) + dot(bl, ih))).astype(BF16)

    @pl.when(tower_ref[0] == 0)
    def _():
        rows_back(((1,), (1,)))

    @pl.when(tower_ref[0] != 0)
    def _():
        rows_back(((1,), (0,)))

    acc = jnp.zeros((32, width), F32)
    for i in range(0, width, 32):
        here = pl.ds(i, 32)
        mine = hi_ref[here, :].astype(F32) + lo_ref[here, :].astype(F32)
        theirs = ohi_ref[here, :].astype(F32) + olo_ref[here, :].astype(F32)
        acc = acc + mine * theirs
    corr_ref[...] = jnp.broadcast_to(jnp.sum(acc), (8, LEAF)) / width


def on_device(embeds, counts):
    own = embeds[0]
    rows, width = own.shape
    blocks = width // LEAF
    half = width // 2
    subs, depths = lax.axis_size("sub"), lax.axis_size("depth")
    sub_index = index_of("sub")
    tower = index_of("tower")
    swap = bit_perm(lax.axis_size("tower"), 1)
    other = lax.ppermute(own, "tower", swap)
    wide = (blocks + 1) * LEAF

    gram = call(
        gram_kernel,
        (full((half // subs, wide), F32),) * subs,
        2,
        1,
        [pltpu.VMEM((rows, width), BF16), pltpu.VMEM((half, wide), F32)],
    )(sub_index, counts, own)
    gram_got = swap_all(gram, "sub")
    cross = call(
        cross_kernel,
        (full((half // subs, width), F32),) * subs,
        3,
        2,
        [pltpu.VMEM((half, width), F32)],
    )(sub_index, tower, counts, own, other)
    cross, gram_got = tie(list(cross), gram_got)

    steps = 1
    direct = half // subs % (8 * depths) == 0
    if direct:
        gram_part = sum_split(gram[0], gram_got, "depth")
        gram_part, cross = tie(gram_part, cross)
        gram_sum = total(gram_part[0], swap_all(gram_part, "depth"))
        cross_part = sum_split(cross[0], swap_all(cross, "sub"), "depth")
        gram_strip = join(spread(gram_sum, "depth"), "depth")
        gram_strip, cross_part = tie(gram_strip, cross_part)
        gram_all = spread(gram_strip, "sub")
        cross_sum = total(cross_part[0], swap_all(cross_part, "depth"))
        cross_sum, gram_all = tie(cross_sum, gram_all)
        cross_got = spread(cross_sum, "depth")
    else:
        gram_all = spread(lax.psum(total(gram[0], gram_got), "depth"), "sub")
        cross_sum = lax.psum(total(cross[0], swap_all(cross, "sub")), "depth")

    square = kept((width, width), F32)
    leaf = kept((LEAF, LEAF), F32)
    work = [pltpu.VMEM((width, LEAF), F32), pltpu.VMEM((LEAF, width), F32)]
    state, sums, pivot = call(
        functools.partial(begin_kernel, steps=steps),
        (square, full((8, width), F32), leaf),
        1,
        subs,
        [pltpu.VMEM((half, wide), F32)] + work,
    )(sub_index, *gram_all)
    cross_strip = join(cross_got, "depth") if direct else cross_sum
    cross_strip, (state, pivot) = tie(cross_strip, (state, pivot))
    other_sums = lax.ppermute(sums, "tower", swap)
    cross_all = spread(cross_strip, "sub")
    work.append(pltpu.VMEM((LEAF, LEAF), F32))
    finish = functools.partial(finish_kernel, first=steps, last=blocks)
    inv = call(finish, square, 0, 2, work)(state, pivot)
    my_half, inv = tie(join(cross_all, "sub"), inv)
    their_half = lax.ppermute(my_half, "tower", swap)

    parts = (full((width, width), BF16),) * 2
    hi, lo = call(regress_kernel, parts, 1, 5)(tower, inv, my_half, their_half, sums, other_sums)
    other_hi = lax.ppermute(hi, "tower", swap)
    other_lo = lax.ppermute(lo, "tower", swap)
    res = call(residual_kernel, kept((rows, width), BF16), 2, 5)(
        tower, counts, own, other, sums, other_sums, hi
    )
    grad, corr = call(gradient_kernel, (full((rows, width), BF16), full((8, LEAF), F32)), 1, 6)(
        tower, res, inv, hi, lo, other_hi, other_lo
    )
    return grad[None], corr[0, 0]


def solution(mesh):
    placed = (P("tower", ("depth", "sub"), None), P(("depth", "sub")))
    return jax.shard_map(
        on_device,
        mesh=mesh,
        in_specs=placed,
        out_specs=(P("tower", ("depth", "sub"), None), P()),
        check_vma=False,
    )
```

```python
import functools

import jax
import jax.numpy as jnp
from jax import lax
from jax.experimental import pallas as pl
from jax.experimental.pallas import tpu as pltpu
from jax.sharding import PartitionSpec as P

REG = 0.001
LEAF = 128
F32 = jnp.float32
BF16 = jnp.bfloat16
VMEM_LIMIT = 24 << 20


def shift_perm(size, apart):
    return [(source, (source + apart) % size) for source in range(size)]


def bit_perm(size, mask):
    return [(source, source ^ mask) for source in range(size)]


def halving_masks(size):
    return [1 << b for b in range(size.bit_length() - 1)]


def swap_all(pieces, axis):
    size = lax.axis_size(axis)
    return [lax.ppermute(pieces[d], axis, bit_perm(size, d)) for d in range(1, size)]


def spread(piece, axis):
    size = lax.axis_size(axis)
    return [piece] + [lax.ppermute(piece, axis, bit_perm(size, d)) for d in range(1, size)]


def index_of(axis):
    return lax.axis_index(axis).astype(jnp.int32).reshape(1)


def tie(first, then):
    return lax.optimization_barrier((first, then))


def sum_split(own, got, axis):
    size = lax.axis_size(axis)
    rows, wide = own.shape
    part = full((rows // size, wide), F32)
    return list(call(split_kernel, (part,) * size, 1, 1 + len(got))(index_of(axis), own, *got))


def total(own, got):
    return call(total_kernel, full(own.shape, F32), 0, 1 + len(got))(own, *got)


def join(pieces, axis):
    rows, wide = pieces[0].shape
    whole = full((rows * len(pieces), wide), F32)
    return call(join_kernel, whole, 1, len(pieces))(index_of(axis), *pieces)


def split(x):
    hi = x.astype(BF16)
    return hi, (x - hi.astype(F32)).astype(BF16)


def dot(a, b, dims=((1,), (0,))):
    return lax.dot_general(a, b, (dims, ((), ())), preferred_element_type=F32)


def wide_left(a):
    hi, lo = split(a)
    return jnp.concatenate([hi, hi, lo], axis=1)


def wide_right(b):
    hi, lo = split(b)
    return jnp.concatenate([hi, lo, hi], axis=0)


def dot3(a, b):
    return dot(wide_left(a), wide_right(b))


def full(shape, dtype):
    return jax.ShapeDtypeStruct(shape, dtype)


def smem():
    return pl.BlockSpec(memory_space=pltpu.SMEM)


def vmem():
    return pl.BlockSpec(memory_space=pltpu.VMEM)


def kept(shape, dtype):
    return pltpu.VMEM(shape, dtype)


def call(kernel, out_shape, n_smem, n_vmem, scratch=()):
    return pl.pallas_call(
        kernel,
        out_shape=out_shape,
        in_specs=[smem()] * n_smem + [vmem()] * n_vmem,
        out_specs=jax.tree.map(lambda _: vmem(), out_shape),
        scratch_shapes=list(scratch),
        compiler_params=pltpu.CompilerParams(vmem_limit_bytes=VMEM_LIMIT),
    )


def split_kernel(me_ref, *refs):
    outs = [ref for ref in refs if ref.shape[0] != refs[0].shape[0]]
    ins = refs[: len(refs) - len(outs)]
    rows = outs[0].shape[0]
    for d, out_ref in enumerate(outs):
        here = pl.ds(pl.multiple_of((me_ref[0] ^ d) * rows, rows), rows)
        acc = ins[0][here, :]
        for ref in ins[1:]:
            acc = acc + ref[here, :]
        out_ref[...] = acc


def total_kernel(*refs):
    acc = refs[0][...]
    for ref in refs[1:-1]:
        acc = acc + ref[...]
    refs[-1][...] = acc


def join_kernel(me_ref, *refs):
    rows = refs[0].shape[0]
    for d, ref in enumerate(refs[:-1]):
        refs[-1][pl.ds(pl.multiple_of((me_ref[0] ^ d) * rows, rows), rows), :] = ref[...]


def deal(me, source_ref, outs):
    rows = outs[0].shape[0]
    for d, out_ref in enumerate(outs):
        out_ref[...] = source_ref[pl.ds(pl.multiple_of((me ^ d) * rows, rows), rows), :]


def gram_kernel(me_ref, count_ref, x_ref, *refs):
    outs, masked_ref, out_ref = refs[:-2], refs[-2], refs[-1]
    rows, width = x_ref.shape
    blocks = width // LEAF
    count = count_ref[0]
    valid = lax.broadcasted_iota(jnp.int32, (rows, LEAF), 0) < count
    for j in range(blocks):
        cols = pl.ds(j * LEAF, LEAF)
        masked_ref[:, cols] = jnp.where(valid, x_ref[:, cols].astype(F32), 0.0).astype(BF16)
    sums = dot(jnp.ones((8, rows), BF16), masked_ref[...])
    sub = lax.broadcasted_iota(jnp.int32, (LEAF, LEAF), 0)
    lane = lax.broadcasted_iota(jnp.int32, (LEAF, LEAF), 1)
    for i in range(blocks):
        wide = (i + 1) * LEAF
        strip = dot(masked_ref[:, i * LEAF : wide], masked_ref[:, :wide], ((0,), (0,)))
        tile = strip[:, i * LEAF :]
        mine = sums[0:1, i * LEAF : wide]
        tile = jnp.where((sub == 0) & (lane > 0), mine, tile)
        last = lane == LEAF - 1
        tile = jnp.where((sub == 1) & last, mine[:, 0:1], tile)
        tile = jnp.where((sub == 2) & last, count.astype(F32), tile)
        if i >= blocks // 2:
            at, row = 0, blocks - 1 - i
        else:
            at, row = (blocks - i) * LEAF, i
        here = pl.ds(row * LEAF, LEAF)
        if i:
            out_ref[here, at : at + i * LEAF] = strip[:, : i * LEAF]
        out_ref[here, at + i * LEAF : at + wide] = tile
    deal(me_ref[0], out_ref, outs)


def cross_kernel(me_ref, tower_ref, count_ref, own_ref, other_ref, *refs):
    outs, out_ref = refs[:-1], refs[-1]
    rows, width = own_ref.shape
    half = width // 2
    valid = lax.broadcasted_iota(jnp.int32, (rows, half), 0) < count_ref[0]

    def part(left_ref, right_ref, first):
        left = left_ref[:, first : first + half]
        left = jnp.where(valid, left.astype(F32), 0.0).astype(BF16)
        out_ref[...] = dot(left, right_ref[...], ((0,), (0,)))

    @pl.when(tower_ref[0] == 0)
    def _():
        part(own_ref, other_ref, 0)

    @pl.when(tower_ref[0] != 0)
    def _():
        part(other_ref, own_ref, half)

    deal(me_ref[0], out_ref, outs)


def inverse_two(a, b, d):
    scale = 1.0 / (a * d - b * b)
    return d * scale, -b * scale, a * scale


def inverse_four(p):
    e00, e01, e11 = inverse_two(p[0][0], p[0][1], p[1][1])
    b00, b01, b10, b11 = p[0][2], p[0][3], p[1][2], p[1][3]
    f00, f01 = e00 * b00 + e01 * b10, e00 * b01 + e01 * b11
    f10, f11 = e01 * b00 + e11 * b10, e01 * b01 + e11 * b11
    g00, g01, g11 = inverse_two(
        p[2][2] - (b00 * f00 + b10 * f10),
        p[2][3] - (b00 * f01 + b10 * f11),
        p[3][3] - (b01 * f01 + b11 * f11),
    )
    h00, h01 = -(f00 * g00 + f01 * g01), -(f00 * g01 + f01 * g11)
    h10, h11 = -(f10 * g00 + f11 * g01), -(f10 * g01 + f11 * g11)
    q00 = e00 - (h00 * f00 + h01 * f01)
    q01 = e01 - (h00 * f10 + h01 * f11)
    q11 = e11 - (h10 * f10 + h11 * f11)
    return [
        [q00, q01, h00, h01],
        [q01, q11, h10, h11],
        [h00, h10, g00, g01],
        [h01, h11, g01, g11],
    ]


PIVOT = 4


def leaf_inverse(block):
    size = block.shape[0]
    tile = (8, size)
    tiles = [block[8 * i : 8 * i + 8, :] for i in range(size // 8)]
    lane = lax.broadcasted_iota(jnp.int32, tile, 1)
    sub = lax.broadcasted_iota(jnp.int32, tile, 0)
    span = range(PIVOT)
    for first in range(0, size, PIVOT):
        home, row = first // 8, first % 8
        rows = [jnp.broadcast_to(tiles[home][row + a : row + a + 1, :], tile) for a in span]
        pivot = [[None] * PIVOT for _ in span]
        for a in span:
            for b in range(a, PIVOT):
                entry = jnp.broadcast_to(rows[a][:, first + b : first + b + 1], tile)
                pivot[a][b] = pivot[b][a] = entry
        cols = [
            [jnp.broadcast_to(t[:, first + b : first + b + 1], tile) for t in tiles] for b in span
        ]
        inv = inverse_four(pivot)
        inside = (lane >= first) & (lane < first + PIVOT)
        rows = [jnp.where(inside, jnp.where(lane == first + a, 1.0, 0.0), rows[a]) for a in span]
        scaled = []
        for a in span:
            acc = inv[a][0] * rows[0]
            for b in range(1, PIVOT):
                acc = acc + inv[a][b] * rows[b]
            scaled.append(acc)
        fresh = []
        for i, old in enumerate(tiles):
            acc = jnp.where(inside, 0.0, old)
            for a in span:
                acc = acc - cols[a][i] * scaled[a]
            if i == home:
                for a in span:
                    acc = jnp.where(sub == row + a, scaled[a], acc)
            fresh.append(acc)
        tiles = fresh
    return jnp.concatenate(tiles, axis=0)


def block(k):
    return pl.ds(pl.multiple_of(k * LEAF, LEAF), LEAF)


def apply_pivot(out_ref, pivot, panel_ref, strip_ref, k, live):
    width = out_ref.shape[0]
    here = block(k)
    sub = lax.broadcasted_iota(jnp.int32, (LEAF, LEAF), 0)
    lane = lax.broadcasted_iota(jnp.int32, (LEAF, LEAF), 1)
    one = jnp.where(sub == lane, 1.0, 0.0)
    old = out_ref[here, :]
    panel_ref[...] = out_ref[:, here] if live is None else jnp.where(live, out_ref[:, here], 0.0)
    out_ref[:, here] = out_ref[:, here] - panel_ref[...]
    out_ref[here, here] = one if live is None else jnp.where(live, one, out_ref[here, here])
    strip = dot3(pivot, out_ref[here, :])
    strip_ref[...] = strip if live is None else jnp.where(live, strip, old)
    panel_ref[here, :] = jnp.zeros((LEAF, LEAF), F32)
    right = wide_right(strip_ref[...])
    for i in range(0, width, 256):
        product = dot(wide_left(panel_ref[i : i + 256, :]), right)
        out_ref[i : i + 256, :] = out_ref[i : i + 256, :] - product
    out_ref[here, :] = strip_ref[...]


def eliminate(out_ref, pivot_ref, panel_ref, strip_ref, first, last):
    blocks = out_ref.shape[0] // LEAF

    def body(ahead, carry):
        live = ahead > 0
        k = jnp.maximum(ahead - 1, 0)
        here, near = block(k), block(ahead)
        pivot = pivot_ref[...]
        side = dot3(out_ref[near, here], dot3(pivot, out_ref[here, near]))
        inv = leaf_inverse(out_ref[near, near] - jnp.where(live, side, 0.0))
        apply_pivot(out_ref, pivot, panel_ref, strip_ref, k, live)
        pivot_ref[...] = inv
        return carry

    lax.fori_loop(first + 1, min(last, blocks - 1) + 1, body, 0)
    if last == blocks:
        apply_pivot(out_ref, pivot_ref[...], panel_ref, strip_ref, blocks - 1, None)


def begin_kernel(me_ref, *refs, steps):
    ins, (out_ref, sums_ref, pivot_ref, packed_ref, panel_ref, strip_ref) = refs[:-6], refs[-6:]
    width = out_ref.shape[0]
    blocks = width // LEAF
    sub = lax.broadcasted_iota(jnp.int32, (LEAF, LEAF), 0)
    lane = lax.broadcasted_iota(jnp.int32, (LEAF, LEAF), 1)
    rows = ins[0].shape[0]
    for d, ref in enumerate(ins):
        packed_ref[pl.ds(pl.multiple_of((me_ref[0] ^ d) * rows, rows), rows), :] = ref[...]

    def packed(i):
        if i >= blocks // 2:
            return pl.ds((blocks - 1 - i) * LEAF, LEAF), 0
        return pl.ds(i * LEAF, LEAF), (blocks - i) * LEAF

    for i in range(blocks):
        here, at = packed(i)
        tile = packed_ref[here, at + i * LEAF : at + (i + 1) * LEAF]
        first = tile[1:2, LEAF - 1 : LEAF]
        mine = jnp.where(lane[0:1] == 0, first, tile[0:1, :])
        sums_ref[0:1, i * LEAF : (i + 1) * LEAF] = mine
        if i == 0:
            count = jnp.broadcast_to(tile[2:3, LEAF - 1 : LEAF], (1, LEAF))
    wide_count = jnp.concatenate([count] * blocks, axis=1)
    sums_ref[1:2, :] = wide_count
    sums_ref[2:3, :] = sums_ref[0:1, :] / wide_count
    sums_ref[3:8, :] = jnp.zeros((5, width), F32)
    scale = 1.0 / (count - 1.0)
    means = sums_ref[2:3, :]
    for i in range(blocks):
        here, at = packed(i)
        own = pl.ds(i * LEAF, LEAF)
        column = jnp.transpose(jnp.broadcast_to(sums_ref[0:1, i * LEAF : (i + 1) * LEAF], (LEAF, LEAF)))
        for j in range(i + 1):
            tile = packed_ref[here, at + j * LEAF : at + (j + 1) * LEAF]
            if j == i:
                tile = jnp.where(sub >= lane, tile, jnp.transpose(tile))
            tile = (tile - column * means[:, j * LEAF : (j + 1) * LEAF]) * scale
            if j == i:
                tile = tile + jnp.where(sub == lane, REG, 0.0)
            out_ref[own, j * LEAF : (j + 1) * LEAF] = tile
            if j < i:
                out_ref[pl.ds(j * LEAF, LEAF), i * LEAF : (i + 1) * LEAF] = jnp.transpose(tile)
    pivot_ref[...] = jnp.zeros((LEAF, LEAF), F32)
    eliminate(out_ref, pivot_ref, panel_ref, strip_ref, -1, steps)


def finish_kernel(in_ref, pivot_in_ref, out_ref, panel_ref, strip_ref, pivot_ref, *, first, last):
    out_ref[...] = in_ref[...]
    pivot_ref[...] = pivot_in_ref[...]
    eliminate(out_ref, pivot_ref, panel_ref, strip_ref, first, last)


def each(rows, part, body):
    def step(i, carry):
        body(pl.ds(pl.multiple_of(i * part, part), part))
        return carry

    lax.fori_loop(0, rows // part, step, 0)


def regress_kernel(
    tower_ref, inv_ref, own_ref, other_ref, sums_ref, osums_ref, hi_ref, lo_ref, parts_h_ref, parts_l_ref
):
    width = inv_ref.shape[0]
    half = width // 2
    scale = 1.0 / (sums_ref[1:2, :] - 1.0)

    def cut(low_ref, high_ref, left_ref, right_mean):
        for ref, base in ((low_ref, 0), (high_ref, half)):

            def strip(here):
                there = pl.ds(pl.multiple_of(here.start + base, LEAF), LEAF)
                column = jnp.transpose(jnp.broadcast_to(left_ref[0:1, there], (LEAF, LEAF)))
                column = jnp.concatenate([column] * (width // LEAF), axis=1)
                hi, lo = split((ref[here, :] - column * right_mean) * scale)
                hi_ref[there, :] = hi
                lo_ref[there, :] = lo

            each(half, LEAF, strip)

    def product(left, right):
        (ah, al), (bh, bl) = left, right
        return dot(ah, bh) + (dot(ah, bl) + dot(al, bh))

    @pl.when(tower_ref[0] == 0)
    def _():
        cut(own_ref, other_ref, sums_ref, osums_ref[2:3, :])
        right = hi_ref[...], lo_ref[...]
        parts_h_ref[...] = right[0]
        parts_l_ref[...] = right[1]

        def strip(here):
            right = parts_h_ref[...], parts_l_ref[...]
            hi, lo = split(product(split(inv_ref[here, :]), right))
            hi_ref[here, :] = hi
            lo_ref[here, :] = lo

        each(width, 256, strip)

    @pl.when(tower_ref[0] != 0)
    def _():
        cut(other_ref, own_ref, osums_ref, sums_ref[2:3, :])
        ih, il = split(inv_ref[...])
        parts_h_ref[...] = ih
        parts_l_ref[...] = il

        def strip(here):
            right = parts_h_ref[...], parts_l_ref[...]
            hi, lo = split(product((hi_ref[here, :], lo_ref[here, :]), right))
            hi_ref[here, :] = hi
            lo_ref[here, :] = lo

        each(width, 256, strip)


def residual_kernel(tower_ref, count_ref, own_ref, other_ref, sums_ref, osums_ref, hi_ref, out_ref):
    rows, width = own_ref.shape

    def fit(dims):
        mean_hi, mean_lo = split(jnp.broadcast_to(sums_ref[2:3, :], (8, width)))
        shift = dot(mean_hi, hi_ref[...], dims) + dot(mean_lo, hi_ref[...], dims)
        shift = shift[0:1, :] - osums_ref[2:3, :]

        def strip(here):
            made = dot(own_ref[here, :], hi_ref[...], dims)
            res = other_ref[here, :].astype(F32) - made + shift
            valid = here.start + lax.broadcasted_iota(jnp.int32, (256, width), 0) < count_ref[0]
            out_ref[here, :] = jnp.where(valid, res, 0.0).astype(BF16)

        each(rows, 256, strip)

    @pl.when(tower_ref[0] == 0)
    def _():
        fit(((1,), (0,)))

    @pl.when(tower_ref[0] != 0)
    def _():
        fit(((1,), (1,)))


def gradient_kernel(
    tower_ref, res_ref, inv_ref, hi_ref, lo_ref, ohi_ref, olo_ref, out_ref, corr_ref, ih_ref, il_ref
):
    rows, width = res_ref.shape

    ih, il = split(inv_ref[...])
    ih_ref[...] = ih
    il_ref[...] = il

    def rows_back(dims):
        def strip(here):
            r = res_ref[here, :]
            bh, bl = split(dot(r, ohi_ref[...], dims) + dot(r, olo_ref[...], dims))
            grad = dot(bh, ih_ref[...]) + (dot(bh, il_ref[...]) + dot(bl, ih_ref[...]))
            out_ref[here, :] = grad.astype(BF16)

        each(rows, 256, strip)

    @pl.when(tower_ref[0] == 0)
    def _():
        rows_back(((1,), (1,)))

    @pl.when(tower_ref[0] != 0)
    def _():
        rows_back(((1,), (0,)))

    def add(i, acc):
        here = pl.ds(pl.multiple_of(i * 16, 16), 16)
        mine = hi_ref[here, :].astype(F32) + lo_ref[here, :].astype(F32)
        theirs = ohi_ref[here, :].astype(F32) + olo_ref[here, :].astype(F32)
        return acc + mine * theirs

    acc = lax.fori_loop(0, width // 16, add, jnp.zeros((16, width), F32))
    corr_ref[...] = jnp.broadcast_to(jnp.sum(acc), (8, LEAF)) / width


def on_device(embeds, counts):
    own = embeds[0]
    rows, width = own.shape
    blocks = width // LEAF
    half = width // 2
    subs, depths = lax.axis_size("sub"), lax.axis_size("depth")
    sub_index = index_of("sub")
    tower = index_of("tower")
    swap = bit_perm(lax.axis_size("tower"), 1)
    other = lax.ppermute(own, "tower", swap)
    wide = (blocks + 1) * LEAF

    gram = call(
        gram_kernel,
        (full((half // subs, wide), F32),) * subs,
        2,
        1,
        [pltpu.VMEM((rows, width), BF16), pltpu.VMEM((half, wide), F32)],
    )(sub_index, counts, own)
    gram_got = swap_all(gram, "sub")
    cross = call(
        cross_kernel,
        (full((half // subs, width), F32),) * subs,
        3,
        2,
        [pltpu.VMEM((half, width), F32)],
    )(sub_index, tower, counts, own, other)
    cross, gram_got = tie(list(cross), gram_got)

    steps = 1
    direct = half // subs % (8 * depths) == 0
    if direct:
        gram_part = sum_split(gram[0], gram_got, "depth")
        gram_part, cross = tie(gram_part, cross)
        gram_sum = total(gram_part[0], swap_all(gram_part, "depth"))
        cross_part = sum_split(cross[0], swap_all(cross, "sub"), "depth")
        gram_strip = join(spread(gram_sum, "depth"), "depth")
        gram_strip, cross_part = tie(gram_strip, cross_part)
        gram_all = spread(gram_strip, "sub")
        cross_sum = total(cross_part[0], swap_all(cross_part, "depth"))
        cross_sum, gram_all = tie(cross_sum, gram_all)
        cross_got = spread(cross_sum, "depth")
    else:
        gram_all = spread(lax.psum(total(gram[0], gram_got), "depth"), "sub")
        cross_sum = lax.psum(total(cross[0], swap_all(cross, "sub")), "depth")

    square = kept((width, width), F32)
    leaf = kept((LEAF, LEAF), F32)
    work = [pltpu.VMEM((width, LEAF), F32), pltpu.VMEM((LEAF, width), F32)]
    state, sums, pivot = call(
        functools.partial(begin_kernel, steps=steps),
        (square, full((8, width), F32), leaf),
        1,
        subs,
        [pltpu.VMEM((half, wide), F32)] + work,
    )(sub_index, *gram_all)
    cross_strip = join(cross_got, "depth") if direct else cross_sum
    cross_strip, (state, pivot) = tie(cross_strip, (state, pivot))
    other_sums = lax.ppermute(sums, "tower", swap)
    cross_all = spread(cross_strip, "sub")
    work.append(pltpu.VMEM((LEAF, LEAF), F32))
    finish = functools.partial(finish_kernel, first=steps, last=blocks)
    inv = call(finish, square, 0, 2, work)(state, pivot)
    my_half, inv = tie(join(cross_all, "sub"), inv)
    their_half = lax.ppermute(my_half, "tower", swap)

    parts = (full((width, width), BF16),) * 2
    hi, lo = call(regress_kernel, parts, 1, 5, [pltpu.VMEM((width, width), BF16)] * 2)(tower, inv, my_half, their_half, sums, other_sums)
    other_hi = lax.ppermute(hi, "tower", swap)
    other_lo = lax.ppermute(lo, "tower", swap)
    res = call(residual_kernel, kept((rows, width), BF16), 2, 5)(
        tower, counts, own, other, sums, other_sums, hi
    )
    outs = full((rows, width), BF16), full((8, LEAF), F32)
    grad, corr = call(gradient_kernel, outs, 1, 6, [pltpu.VMEM((width, width), BF16)] * 2)(
        tower, res, inv, hi, lo, other_hi, other_lo
    )
    return grad[None], corr[0, 0]


def solution(mesh):
    placed = (P("tower", ("depth", "sub"), None), P(("depth", "sub")))
    return jax.shard_map(
        on_device,
        mesh=mesh,
        in_specs=placed,
        out_specs=(P("tower", ("depth", "sub"), None), P()),
        check_vma=False,
    )
```

```python
import functools

import jax
import jax.numpy as jnp
from jax import lax
from jax.experimental import pallas as pl
from jax.experimental.pallas import tpu as pltpu
from jax.sharding import PartitionSpec as P


REG = 0.001
LEAF = 128
F32 = jnp.float32
BF16 = jnp.bfloat16
VMEM_LIMIT = 24 << 20


def bit_perm(size, mask):
    return [(source, source ^ mask) for source in range(size)]


def swap_all(pieces, axis):
    size = lax.axis_size(axis)
    return [lax.ppermute(pieces[d], axis, bit_perm(size, d)) for d in range(1, size)]


def spread(piece, axis):
    size = lax.axis_size(axis)
    return [piece] + [lax.ppermute(piece, axis, bit_perm(size, d)) for d in range(1, size)]


def index_of(axis):
    return lax.axis_index(axis).astype(jnp.int32).reshape(1)


def tie(first, then):
    return lax.optimization_barrier((first, then))


def sum_split(own, got, axis):
    size = lax.axis_size(axis)
    rows, wide = own.shape
    part = full((rows // size, wide), F32)
    return list(call(split_kernel, (part,) * size, 1, 1 + len(got))(index_of(axis), own, *got))


def total(own, got):
    return call(total_kernel, full(own.shape, F32), 0, 1 + len(got))(own, *got)


def join(pieces, axis):
    rows, wide = pieces[0].shape
    whole = full((rows * len(pieces), wide), F32)
    return call(join_kernel, whole, 1, len(pieces))(index_of(axis), *pieces)


def split(x):
    hi = x.astype(BF16)
    return hi, (x - hi.astype(F32)).astype(BF16)


def dot(a, b, dims=((1,), (0,))):
    return lax.dot_general(a, b, (dims, ((), ())), preferred_element_type=F32)


def wide_left(a):
    hi, lo = split(a)
    return jnp.concatenate([hi, hi, lo], axis=1)


def wide_right(b):
    hi, lo = split(b)
    return jnp.concatenate([hi, lo, hi], axis=0)


def dot3(a, b):
    return dot(wide_left(a), wide_right(b))


def full(shape, dtype):
    return jax.ShapeDtypeStruct(shape, dtype)


def smem():
    return pl.BlockSpec(memory_space=pltpu.SMEM)


def vmem():
    return pl.BlockSpec(memory_space=pltpu.VMEM)


def kept(shape, dtype):
    return pltpu.VMEM(shape, dtype)


def call(kernel, out_shape, n_smem, n_vmem, scratch=()):
    return pl.pallas_call(
        kernel,
        out_shape=out_shape,
        in_specs=[smem()] * n_smem + [vmem()] * n_vmem,
        out_specs=jax.tree.map(lambda _: vmem(), out_shape),
        scratch_shapes=list(scratch),
        compiler_params=pltpu.CompilerParams(vmem_limit_bytes=VMEM_LIMIT),
    )


def split_kernel(me_ref, *refs):
    outs = [ref for ref in refs if ref.shape[0] != refs[0].shape[0]]
    ins = refs[: len(refs) - len(outs)]
    rows = outs[0].shape[0]
    for d, out_ref in enumerate(outs):
        here = pl.ds(pl.multiple_of((me_ref[0] ^ d) * rows, rows), rows)
        acc = ins[0][here, :]
        for ref in ins[1:]:
            acc = acc + ref[here, :]
        out_ref[...] = acc


def total_kernel(*refs):
    acc = refs[0][...]
    for ref in refs[1:-1]:
        acc = acc + ref[...]
    refs[-1][...] = acc


def join_kernel(me_ref, *refs):
    rows = refs[0].shape[0]
    for d, ref in enumerate(refs[:-1]):
        refs[-1][pl.ds(pl.multiple_of((me_ref[0] ^ d) * rows, rows), rows), :] = ref[...]


def deal(me, source_ref, outs):
    rows = outs[0].shape[0]
    for d, out_ref in enumerate(outs):
        out_ref[...] = source_ref[pl.ds(pl.multiple_of((me ^ d) * rows, rows), rows), :]


def gram_kernel(me_ref, count_ref, x_ref, *refs):
    outs, masked_ref, out_ref = refs[:-2], refs[-2], refs[-1]
    rows, width = x_ref.shape
    blocks = width // LEAF
    count = count_ref[0]
    valid = lax.broadcasted_iota(jnp.int32, (rows, LEAF), 0) < count
    for j in range(blocks):
        cols = pl.ds(j * LEAF, LEAF)
        masked_ref[:, cols] = jnp.where(valid, x_ref[:, cols].astype(F32), 0.0).astype(BF16)
    sums = dot(jnp.ones((8, rows), BF16), masked_ref[...])
    sub = lax.broadcasted_iota(jnp.int32, (LEAF, LEAF), 0)
    lane = lax.broadcasted_iota(jnp.int32, (LEAF, LEAF), 1)
    for i in range(blocks):
        wide = (i + 1) * LEAF
        strip = dot(masked_ref[:, i * LEAF : wide], masked_ref[:, :wide], ((0,), (0,)))
        tile = strip[:, i * LEAF :]
        mine = sums[0:1, i * LEAF : wide]
        tile = jnp.where((sub == 0) & (lane > 0), mine, tile)
        last = lane == LEAF - 1
        tile = jnp.where((sub == 1) & last, mine[:, 0:1], tile)
        tile = jnp.where((sub == 2) & last, count.astype(F32), tile)
        if i >= blocks // 2:
            at, row = 0, blocks - 1 - i
        else:
            at, row = (blocks - i) * LEAF, i
        here = pl.ds(row * LEAF, LEAF)
        if i:
            out_ref[here, at : at + i * LEAF] = strip[:, : i * LEAF]
        out_ref[here, at + i * LEAF : at + wide] = tile
    deal(me_ref[0], out_ref, outs)


def cross_kernel(me_ref, tower_ref, count_ref, own_ref, other_ref, *refs):
    outs, out_ref = refs[:-1], refs[-1]
    rows, width = own_ref.shape
    half = width // 2
    valid = lax.broadcasted_iota(jnp.int32, (rows, half), 0) < count_ref[0]

    def part(left_ref, right_ref, first):
        left = left_ref[:, first : first + half]
        left = jnp.where(valid, left.astype(F32), 0.0).astype(BF16)
        out_ref[...] = dot(left, right_ref[...], ((0,), (0,)))

    @pl.when(tower_ref[0] == 0)
    def _():
        part(own_ref, other_ref, 0)

    @pl.when(tower_ref[0] != 0)
    def _():
        part(other_ref, own_ref, half)

    deal(me_ref[0], out_ref, outs)


def inverse_two(a, b, d):
    scale = 1.0 / (a * d - b * b)
    return d * scale, -b * scale, a * scale


def inverse_four(p):
    e00, e01, e11 = inverse_two(p[0][0], p[0][1], p[1][1])
    b00, b01, b10, b11 = p[0][2], p[0][3], p[1][2], p[1][3]
    f00, f01 = e00 * b00 + e01 * b10, e00 * b01 + e01 * b11
    f10, f11 = e01 * b00 + e11 * b10, e01 * b01 + e11 * b11
    g00, g01, g11 = inverse_two(
        p[2][2] - (b00 * f00 + b10 * f10),
        p[2][3] - (b00 * f01 + b10 * f11),
        p[3][3] - (b01 * f01 + b11 * f11),
    )
    h00, h01 = -(f00 * g00 + f01 * g01), -(f00 * g01 + f01 * g11)
    h10, h11 = -(f10 * g00 + f11 * g01), -(f10 * g01 + f11 * g11)
    q00 = e00 - (h00 * f00 + h01 * f01)
    q01 = e01 - (h00 * f10 + h01 * f11)
    q11 = e11 - (h10 * f10 + h11 * f11)
    return [
        [q00, q01, h00, h01],
        [q01, q11, h10, h11],
        [h00, h10, g00, g01],
        [h01, h11, g01, g11],
    ]


PIVOT = 4


def leaf_inverse(block):
    size = block.shape[0]
    tile = (8, size)
    tiles = [block[8 * i : 8 * i + 8, :] for i in range(size // 8)]
    lane = lax.broadcasted_iota(jnp.int32, tile, 1)
    sub = lax.broadcasted_iota(jnp.int32, tile, 0)
    span = range(PIVOT)
    for first in range(0, size, PIVOT):
        home, row = first // 8, first % 8
        rows = [jnp.broadcast_to(tiles[home][row + a : row + a + 1, :], tile) for a in span]
        pivot = [[None] * PIVOT for _ in span]
        for a in span:
            for b in range(a, PIVOT):
                entry = jnp.broadcast_to(rows[a][:, first + b : first + b + 1], tile)
                pivot[a][b] = pivot[b][a] = entry
        cols = [
            [jnp.broadcast_to(t[:, first + b : first + b + 1], tile) for t in tiles] for b in span
        ]
        inv = inverse_four(pivot)
        inside = (lane >= first) & (lane < first + PIVOT)
        rows = [jnp.where(inside, jnp.where(lane == first + a, 1.0, 0.0), rows[a]) for a in span]
        scaled = []
        for a in span:
            acc = inv[a][0] * rows[0]
            for b in range(1, PIVOT):
                acc = acc + inv[a][b] * rows[b]
            scaled.append(acc)
        fresh = []
        for i, old in enumerate(tiles):
            acc = jnp.where(inside, 0.0, old)
            for a in span:
                acc = acc - cols[a][i] * scaled[a]
            if i == home:
                for a in span:
                    acc = jnp.where(sub == row + a, scaled[a], acc)
            fresh.append(acc)
        tiles = fresh
    return jnp.concatenate(tiles, axis=0)


def block(k):
    return pl.ds(pl.multiple_of(k * LEAF, LEAF), LEAF)


def apply_pivot(out_ref, pivot, panel_ref, strip_ref, k, live):
    width = out_ref.shape[0]
    here = block(k)
    sub = lax.broadcasted_iota(jnp.int32, (LEAF, LEAF), 0)
    lane = lax.broadcasted_iota(jnp.int32, (LEAF, LEAF), 1)
    one = jnp.where(sub == lane, 1.0, 0.0)
    old = out_ref[here, :]
    panel_ref[...] = out_ref[:, here] if live is None else jnp.where(live, out_ref[:, here], 0.0)
    out_ref[:, here] = out_ref[:, here] - panel_ref[...]
    out_ref[here, here] = one if live is None else jnp.where(live, one, out_ref[here, here])
    strip = dot3(pivot, out_ref[here, :])
    strip_ref[...] = strip if live is None else jnp.where(live, strip, old)
    panel_ref[here, :] = jnp.zeros((LEAF, LEAF), F32)
    right = wide_right(strip_ref[...])
    for i in range(0, width, 256):
        product = dot(wide_left(panel_ref[i : i + 256, :]), right)
        out_ref[i : i + 256, :] = out_ref[i : i + 256, :] - product
    out_ref[here, :] = strip_ref[...]


def eliminate(out_ref, pivot_ref, panel_ref, strip_ref, first, last):
    blocks = out_ref.shape[0] // LEAF

    def body(ahead, carry):
        live = ahead > 0
        k = jnp.maximum(ahead - 1, 0)
        here, near = block(k), block(ahead)
        pivot = pivot_ref[...]
        side = dot3(out_ref[near, here], dot3(pivot, out_ref[here, near]))
        inv = leaf_inverse(out_ref[near, near] - jnp.where(live, side, 0.0))
        apply_pivot(out_ref, pivot, panel_ref, strip_ref, k, live)
        pivot_ref[...] = inv
        return carry

    lax.fori_loop(first + 1, min(last, blocks - 1) + 1, body, 0)
    if last == blocks:
        apply_pivot(out_ref, pivot_ref[...], panel_ref, strip_ref, blocks - 1, None)


def begin_kernel(me_ref, *refs, steps):
    ins, (out_ref, sums_ref, pivot_ref, packed_ref, panel_ref, strip_ref) = refs[:-6], refs[-6:]
    width = out_ref.shape[0]
    blocks = width // LEAF
    sub = lax.broadcasted_iota(jnp.int32, (LEAF, LEAF), 0)
    lane = lax.broadcasted_iota(jnp.int32, (LEAF, LEAF), 1)
    rows = ins[0].shape[0]
    for d, ref in enumerate(ins):
        packed_ref[pl.ds(pl.multiple_of((me_ref[0] ^ d) * rows, rows), rows), :] = ref[...]

    def packed(i):
        if i >= blocks // 2:
            return pl.ds((blocks - 1 - i) * LEAF, LEAF), 0
        return pl.ds(i * LEAF, LEAF), (blocks - i) * LEAF

    for i in range(blocks):
        here, at = packed(i)
        tile = packed_ref[here, at + i * LEAF : at + (i + 1) * LEAF]
        first = tile[1:2, LEAF - 1 : LEAF]
        mine = jnp.where(lane[0:1] == 0, first, tile[0:1, :])
        sums_ref[0:1, i * LEAF : (i + 1) * LEAF] = mine
        if i == 0:
            count = jnp.broadcast_to(tile[2:3, LEAF - 1 : LEAF], (1, LEAF))
    wide_count = jnp.concatenate([count] * blocks, axis=1)
    sums_ref[1:2, :] = wide_count
    sums_ref[2:3, :] = sums_ref[0:1, :] / wide_count
    sums_ref[3:8, :] = jnp.zeros((5, width), F32)
    scale = 1.0 / (count - 1.0)
    means = sums_ref[2:3, :]
    for i in range(blocks):
        here, at = packed(i)
        own = pl.ds(i * LEAF, LEAF)
        column = jnp.transpose(jnp.broadcast_to(sums_ref[0:1, i * LEAF : (i + 1) * LEAF], (LEAF, LEAF)))
        for j in range(i + 1):
            tile = packed_ref[here, at + j * LEAF : at + (j + 1) * LEAF]
            if j == i:
                tile = jnp.where(sub >= lane, tile, jnp.transpose(tile))
            tile = (tile - column * means[:, j * LEAF : (j + 1) * LEAF]) * scale
            if j == i:
                tile = tile + jnp.where(sub == lane, REG, 0.0)
            out_ref[own, j * LEAF : (j + 1) * LEAF] = tile
            if j < i:
                out_ref[pl.ds(j * LEAF, LEAF), i * LEAF : (i + 1) * LEAF] = jnp.transpose(tile)
    pivot_ref[...] = jnp.zeros((LEAF, LEAF), F32)
    eliminate(out_ref, pivot_ref, panel_ref, strip_ref, -1, steps)


def finish_kernel(in_ref, pivot_in_ref, out_ref, panel_ref, strip_ref, pivot_ref, *, first, last):
    out_ref[...] = in_ref[...]
    pivot_ref[...] = pivot_in_ref[...]
    eliminate(out_ref, pivot_ref, panel_ref, strip_ref, first, last)


def each(rows, part, body):
    def step(i, carry):
        body(pl.ds(pl.multiple_of(i * part, part), part))
        return carry

    lax.fori_loop(0, rows // part, step, 0)


def regress_kernel(
    tower_ref, inv_ref, own_ref, other_ref, sums_ref, osums_ref, hi_ref, lo_ref, parts_h_ref, parts_l_ref
):
    width = inv_ref.shape[0]
    half = width // 2
    scale = 1.0 / (sums_ref[1:2, :] - 1.0)

    def cut(low_ref, high_ref, left_ref, right_mean):
        for ref, base in ((low_ref, 0), (high_ref, half)):

            def strip(here):
                there = pl.ds(pl.multiple_of(here.start + base, LEAF), LEAF)
                column = jnp.transpose(jnp.broadcast_to(left_ref[0:1, there], (LEAF, LEAF)))
                column = jnp.concatenate([column] * (width // LEAF), axis=1)
                hi, lo = split((ref[here, :] - column * right_mean) * scale)
                hi_ref[there, :] = hi
                lo_ref[there, :] = lo

            each(half, LEAF, strip)

    def product(left, right):
        (ah, al), (bh, bl) = left, right
        return dot(ah, bh) + (dot(ah, bl) + dot(al, bh))

    @pl.when(tower_ref[0] == 0)
    def _():
        cut(own_ref, other_ref, sums_ref, osums_ref[2:3, :])
        right = hi_ref[...], lo_ref[...]
        parts_h_ref[...] = right[0]
        parts_l_ref[...] = right[1]

        def strip(here):
            right = parts_h_ref[...], parts_l_ref[...]
            hi, lo = split(product(split(inv_ref[here, :]), right))
            hi_ref[here, :] = hi
            lo_ref[here, :] = lo

        each(width, 256, strip)

    @pl.when(tower_ref[0] != 0)
    def _():
        cut(other_ref, own_ref, osums_ref, sums_ref[2:3, :])
        ih, il = split(inv_ref[...])
        parts_h_ref[...] = ih
        parts_l_ref[...] = il

        def strip(here):
            right = parts_h_ref[...], parts_l_ref[...]
            hi, lo = split(product((hi_ref[here, :], lo_ref[here, :]), right))
            hi_ref[here, :] = hi
            lo_ref[here, :] = lo

        each(width, 256, strip)


def residual_kernel(tower_ref, count_ref, own_ref, other_ref, sums_ref, osums_ref, hi_ref, out_ref):
    rows, width = own_ref.shape

    def fit(dims):
        mean_hi, mean_lo = split(jnp.broadcast_to(sums_ref[2:3, :], (8, width)))
        shift = dot(mean_hi, hi_ref[...], dims) + dot(mean_lo, hi_ref[...], dims)
        shift = shift[0:1, :] - osums_ref[2:3, :]

        def strip(here):
            made = dot(own_ref[here, :], hi_ref[...], dims)
            res = other_ref[here, :].astype(F32) - made + shift
            valid = here.start + lax.broadcasted_iota(jnp.int32, (256, width), 0) < count_ref[0]
            out_ref[here, :] = jnp.where(valid, res, 0.0).astype(BF16)

        each(rows, 256, strip)

    @pl.when(tower_ref[0] == 0)
    def _():
        fit(((1,), (0,)))

    @pl.when(tower_ref[0] != 0)
    def _():
        fit(((1,), (1,)))


def gradient_kernel(
    tower_ref, res_ref, inv_ref, hi_ref, lo_ref, ohi_ref, olo_ref, out_ref, corr_ref, ih_ref, il_ref
):
    rows, width = res_ref.shape

    ih, il = split(inv_ref[...])
    ih_ref[...] = ih
    il_ref[...] = il

    def rows_back(dims):
        def strip(here):
            r = res_ref[here, :]
            bh, bl = split(dot(r, ohi_ref[...], dims) + dot(r, olo_ref[...], dims))
            grad = dot(bh, ih_ref[...]) + (dot(bh, il_ref[...]) + dot(bl, ih_ref[...]))
            out_ref[here, :] = grad.astype(BF16)

        each(rows, 256, strip)

    @pl.when(tower_ref[0] == 0)
    def _():
        rows_back(((1,), (1,)))

    @pl.when(tower_ref[0] != 0)
    def _():
        rows_back(((1,), (0,)))

    def add(i, acc):
        here = pl.ds(pl.multiple_of(i * 16, 16), 16)
        mine = hi_ref[here, :].astype(F32) + lo_ref[here, :].astype(F32)
        theirs = ohi_ref[here, :].astype(F32) + olo_ref[here, :].astype(F32)
        return acc + mine * theirs

    acc = lax.fori_loop(0, width // 16, add, jnp.zeros((16, width), F32))
    corr_ref[...] = jnp.broadcast_to(jnp.sum(acc), (8, LEAF)) / width


def on_device(embeds, counts):
    own = embeds[0]
    rows, width = own.shape
    blocks = width // LEAF
    half = width // 2
    subs, depths = lax.axis_size("sub"), lax.axis_size("depth")
    sub_index = index_of("sub")
    tower = index_of("tower")
    swap = bit_perm(lax.axis_size("tower"), 1)
    other = lax.ppermute(own, "tower", swap)
    wide = (blocks + 1) * LEAF

    gram = call(
        gram_kernel,
        (full((half // subs, wide), F32),) * subs,
        2,
        1,
        [pltpu.VMEM((rows, width), BF16), pltpu.VMEM((half, wide), F32)],
    )(sub_index, counts, own)
    gram_got = swap_all(gram, "sub")
    cross = call(
        cross_kernel,
        (full((half // subs, width), F32),) * subs,
        3,
        2,
        [pltpu.VMEM((half, width), F32)],
    )(sub_index, tower, counts, own, other)
    cross, gram_got = tie(list(cross), gram_got)

    steps = 1
    direct = half // subs % (8 * depths) == 0
    if direct:
        gram_part = sum_split(gram[0], gram_got, "depth")
        gram_part, cross = tie(gram_part, cross)
        gram_got = swap_all(gram_part, "depth")
        cross_got = swap_all(cross, "sub")
        gram_sum = total(gram_part[0], gram_got)
        cross_part = sum_split(cross[0], cross_got, "depth")
        gram_strip = join(spread(gram_sum, "depth"), "depth")
        gram_strip, cross_part = tie(gram_strip, cross_part)
        gram_all = spread(gram_strip, "sub")
        cross_sum = total(cross_part[0], swap_all(cross_part, "depth"))
        cross_sum, gram_all = tie(cross_sum, gram_all)
        cross_got = spread(cross_sum, "depth")
    else:
        gram_all = spread(lax.psum(total(gram[0], gram_got), "depth"), "sub")
        cross_sum = lax.psum(total(cross[0], swap_all(cross, "sub")), "depth")

    square = kept((width, width), F32)
    leaf = kept((LEAF, LEAF), F32)
    work = [pltpu.VMEM((width, LEAF), F32), pltpu.VMEM((LEAF, width), F32)]
    state, sums, pivot = call(
        functools.partial(begin_kernel, steps=steps),
        (square, full((8, width), F32), leaf),
        1,
        subs,
        [pltpu.VMEM((half, wide), F32)] + work,
    )(sub_index, *gram_all)
    cross_strip = join(cross_got, "depth") if direct else cross_sum
    cross_strip, (state, pivot) = tie(cross_strip, (state, pivot))
    other_sums = lax.ppermute(sums, "tower", swap)
    cross_all = spread(cross_strip, "sub")
    work.append(pltpu.VMEM((LEAF, LEAF), F32))
    finish = functools.partial(finish_kernel, first=steps, last=blocks)
    inv = call(finish, square, 0, 2, work)(state, pivot)
    my_half, inv = tie(join(cross_all, "sub"), inv)
    their_half = lax.ppermute(my_half, "tower", swap)

    parts = (full((width, width), BF16),) * 2
    hi, lo = call(regress_kernel, parts, 1, 5, [pltpu.VMEM((width, width), BF16)] * 2)(tower, inv, my_half, their_half, sums, other_sums)
    other_hi = lax.ppermute(hi, "tower", swap)
    other_lo = lax.ppermute(lo, "tower", swap)
    res = call(residual_kernel, kept((rows, width), BF16), 2, 5)(
        tower, counts, own, other, sums, other_sums, hi
    )
    outs = full((rows, width), BF16), full((8, LEAF), F32)
    grad, corr = call(gradient_kernel, outs, 1, 6, [pltpu.VMEM((width, width), BF16)] * 2)(
        tower, res, inv, hi, lo, other_hi, other_lo
    )
    return grad[None], corr[0, 0]


def solution(mesh):
    placed = (P("tower", ("depth", "sub"), None), P(("depth", "sub")))
    return jax.shard_map(
        on_device,
        mesh=mesh,
        in_specs=placed,
        out_specs=(P("tower", ("depth", "sub"), None), P()),
        check_vma=False,
    )
```
